256 devices in a mesh: rep: 8 (over x_lo, y), own: 32 (over z, x_hi, core).
Axes of the slice: x: 4 (x_hi: 2, x_lo: 2; x = x_hi * 2 + x_lo), y: 4, z: 8, core: 2. Of those that a mesh axis runs over, the one named last changes fastest.
Arguments:
- local_dense: bfloat16 [8, 1024, 187, 128], P('rep', 'own')
- owner_list: int32 [187], replicated, may hold values from 0 to 31, as said below
- anchor_slots: float32 [32, 1024, 12, 128], P('own', None, None, 'rep'), may hold values from -100 to 100
- moment_slots: float32 [32, 1024, 12, 128], P('own', None, None, 'rep'), may hold values from -3 to 3
- local_embed: bfloat16 [8, 26624, 1024], P('rep', 'own'), may hold values from -6 to 6
- anchor_embed: float32 [26624, 1024], P('own', 'rep'), may hold values from -6 to 6
- moment_embed: float32 [26624, 64], P('own'), may hold values from -3 to 3
- projection: bfloat16 [1024, 64], replicated, may hold values from -0.1875 to 0.1875
Outputs:
- dense_weights: bfloat16 [1024, 187, 128], P('own')
- anchor_slots_new: float32 [32, 1024, 12, 128], P('own', None, None, 'rep')
- moment_slots_new: float32 [32, 1024, 12, 128], P('own', None, None, 'rep')
- embed_weights: bfloat16 [26624, 1024], P('own')
- anchor_embed_new: float32 [26624, 1024], P('own', 'rep')
- moment_embed_new: float32 [26624, 64], P('own')
The draws below stay inside these ranges and needn't reach their ends.
Inputs may be any that keep to these rules, and one draw needn't show every extreme that they name: `owner_list`: each owner holds at most 12 blocks, and some owner holds exactly 12.
All inputs are finite; a program needn't handle non-finite values.
Results may differ from the reference program's by a relative error of at most 0.015.
Values may be sent and summed in bfloat16 or wider, within the bound.
A program may use at most 128 MiB of HBM per device.

```python
import math
import jax
import jax.numpy as jnp
from jax import lax

D = 1024
VOCAB = 26624
RANK = 64
LAYERS = 2
BLOCK = 64
SLAB = 128
UNITS = 187
CAP = 12
REPS = 8
N_OWN = 32


def column_ramp(count, top):
    steps = jnp.arange(count, dtype=jnp.float32) / max(count - 1, 1)
    return jnp.exp(steps * math.log(top))


def draw_owner_list(key, part):
    first_key, second_key, third_key = jax.random.split(key, 3)
    slot_total = N_OWN * CAP
    heavy_owner = jax.random.randint(first_key, (), 0, N_OWN)
    shuffled = jax.random.permutation(second_key, slot_total).astype(jnp.int32)
    slot_index = jnp.arange(slot_total, dtype=jnp.int32)
    slot_score = jnp.where(slot_index // CAP == heavy_owner, -1 - slot_index, shuffled)
    chosen = jnp.argsort(slot_score, stable=True)[:UNITS].astype(jnp.int32)
    unit_order = jax.random.permutation(third_key, UNITS)
    return (chosen[unit_order] // CAP).astype(jnp.int32)


def draw_local_dense(key, part):
    first_key, second_key, third_key = jax.random.split(key, 3)
    low = math.log(0.5)
    high = math.log(5.0)
    unit_scale = jnp.exp(jax.random.uniform(first_key, (UNITS,), jnp.float32, low, high))
    row_scale = jnp.exp(jax.random.uniform(second_key, (D,), jnp.float32, low, high))
    shape_full = (REPS, D, UNITS, LAYERS * BLOCK)
    noise_base = jax.random.normal(third_key, shape_full, jnp.float32)
    ramp = column_ramp(LAYERS * BLOCK, 6.0)
    values = noise_base * row_scale[None, :, None, None] * unit_scale[None, None, :, None] * ramp[None, None, None, :]
    return values.astype(jnp.bfloat16)


def draw_anchor_slots(key, part):
    first_key = jax.random.fold_in(jax.random.fold_in(key, 7), 0)
    shape_full = (N_OWN, D, CAP, LAYERS * BLOCK)
    noise_base = jnp.clip(jax.random.normal(first_key, shape_full, jnp.float32), -6.0, 6.0)
    ramp = column_ramp(LAYERS * BLOCK, 6.0)
    return (noise_base * ramp[None, None, None, :]).astype(jnp.float32)


def steps_of(own_key, extent, cuts, least, largest):
    loudness = 1.0
    for axis_at, shards_of in cuts:
        steps = jax.random.uniform(jax.random.fold_in(jax.random.fold_in(own_key, 6), axis_at), (shards_of,), jnp.float32, least / len(cuts), largest / len(cuts))
        loudness = loudness * jnp.repeat(jnp.exp(steps), extent[axis_at] // shards_of).reshape((-1,) + (1,) * (len(extent) - 1 - axis_at))
    return loudness


def bell_draw(own_key, extent, deviation, bound, cuts=(), kind=jnp.bfloat16):
    entries = deviation * jax.random.normal(own_key, extent, jnp.float32)
    if cuts:
        entries = entries * steps_of(own_key, extent, cuts, -0.22, 0.18)
    return jnp.clip(entries, -bound, bound).astype(kind)


def setup_inputs(seed: int = 0) -> dict:
    streams_of = jax.random.split(jax.random.key(seed), 9)
    local_dense = draw_local_dense(jax.random.fold_in(streams_of[8], 71), 0)
    owner_list = draw_owner_list(jax.random.fold_in(streams_of[8], 71), 0)
    anchor_slots = draw_anchor_slots(jax.random.fold_in(streams_of[8], 71), 0)
    moment_slots = bell_draw(streams_of[3], (N_OWN, D, CAP, SLAB), 0.5, 3.0, ((0, 32), (3, 8)), jnp.float32)
    local_embed = bell_draw(streams_of[4], (REPS, VOCAB, D), 1.0, 6.0, ((0, 8), (1, 32)))
    anchor_embed = bell_draw(streams_of[5], (VOCAB, D), 1.0, 6.0, ((0, 32), (1, 8)), jnp.float32)
    moment_embed = bell_draw(streams_of[6], (VOCAB, RANK), 0.5, 3.0, ((0, 32),), jnp.float32)
    projection = bell_draw(streams_of[7], (D, RANK), D ** -0.5, 0.1875)
    return dict(local_dense=local_dense, owner_list=owner_list, anchor_slots=anchor_slots, moment_slots=moment_slots, local_embed=local_embed, anchor_embed=anchor_embed, moment_embed=moment_embed, projection=projection)


OUTER_MOMENTUM = 0.9
OUTER_RATE = 0.7
CLIP_RMS = 2.0
EPSILON = 1e-06

def slot_tables(owner_list):
    onehot = (owner_list[:, None] == jnp.arange(N_OWN, dtype=jnp.int32)[None, :]).astype(jnp.int32)
    before = jnp.cumsum(onehot, axis=0) - onehot
    slot_rank = lax.optimization_barrier(jnp.sum(before * onehot, axis=1)).astype(jnp.int32)
    flat_index = (owner_list * CAP + slot_rank).astype(jnp.int32)
    matches = (jnp.arange(N_OWN * CAP, dtype=jnp.int32)[:, None] == flat_index[None, :]).astype(jnp.int32)
    slot_units = lax.optimization_barrier(jnp.sum(matches * jnp.arange(UNITS, dtype=jnp.int32)[None, :], axis=1)).astype(jnp.int32)
    live_slots = lax.optimization_barrier(jnp.sum(matches, axis=1))
    return (flat_index, slot_units, live_slots)

def reference(local_dense, owner_list, anchor_slots, moment_slots, local_embed, anchor_embed, moment_embed, projection):
    running = jnp.zeros(local_dense.shape[1:], jnp.float32)
    for group_idx in range(REPS):
        running = running + local_dense[group_idx].astype(jnp.float32)
    flat_index, slot_units, live_slots = slot_tables(owner_list)
    picked = jnp.take(running, slot_units, axis=1)
    picked = picked.reshape(D, N_OWN, CAP, SLAB).transpose(1, 0, 2, 3)
    live_share = live_slots.astype(jnp.float32).reshape(N_OWN, 1, CAP, 1)
    change = anchor_slots - picked / REPS
    squares = lax.optimization_barrier(jnp.sum(change * change, axis=(1, 3), keepdims=True))
    root_mean = jnp.sqrt(squares / (D * SLAB) + EPSILON)
    clipped = change * jnp.minimum(1.0, CLIP_RMS / root_mean)
    moment_new = live_share * (OUTER_MOMENTUM * moment_slots + clipped)
    anchor_new = live_share * (anchor_slots - OUTER_RATE * (clipped + OUTER_MOMENTUM * moment_new))
    rounded = anchor_new.astype(jnp.bfloat16).transpose(1, 0, 2, 3).reshape(D, N_OWN * CAP, SLAB)
    dense_weights = jnp.take(rounded, flat_index, axis=1)
    embed_total = jnp.zeros(anchor_embed.shape, jnp.float32)
    for group_idx in range(REPS):
        embed_total = embed_total + local_embed[group_idx].astype(jnp.float32)
    embed_change = anchor_embed - embed_total / REPS
    proj_full = projection.astype(jnp.float32)
    compressed = jnp.dot(embed_change, proj_full, precision=lax.Precision.HIGHEST)
    moment_embed_new = OUTER_MOMENTUM * moment_embed + compressed
    anchor_embed_new = anchor_embed - OUTER_RATE * jnp.dot(compressed + OUTER_MOMENTUM * moment_embed_new, proj_full.T, precision=lax.Precision.HIGHEST)
    embed_weights = anchor_embed_new.astype(jnp.bfloat16)
    return (dense_weights, anchor_new, moment_new, embed_weights, anchor_embed_new, moment_embed_new)
```

```python
import functools

import jax
import jax.numpy as jnp
from jax import lax
from jax.experimental import pallas as pl
from jax.experimental.pallas import tpu as pltpu
from jax.sharding import PartitionSpec as P

OUTER_MOMENTUM = 0.9
OUTER_RATE = 0.7
CLIP_RMS = 2.0
EPSILON = 1e-06
MESH = pl.DeviceIdType.MESH
F32 = jnp.float32
BF16 = jnp.bfloat16
HIGHEST = lax.Precision.HIGHEST


def iota(shape, axis):
    return lax.broadcasted_iota(jnp.int32, shape, axis)


def onehot(condition):
    return jnp.where(condition, 1.0, 0.0).astype(BF16)


def kernel(
    dims,
    dense_ref,
    owner_row_ref,
    owner_col_ref,
    anchor_ref,
    moment_ref,
    embed_ref,
    anchor_embed_ref,
    moment_embed_ref,
    projection_ref,
    dense_out,
    anchor_out,
    moment_out,
    embed_out,
    anchor_embed_out,
    moment_embed_out,
    stored,
    wide,
    share_send,
    share_recv,
    summed,
    slot_pick,
    unit_pick,
    to_rows,
    from_rows,
    out_send,
    out_recv,
    slots_f32,
    spread,
    change,
    squares_send,
    squares_recv,
    back_send,
    back_recv,
    column_send,
    column_recv,
    part_send,
    part_recv,
    part_sum,
    compressed,
    embed_send,
    share_sems,
    out_sems,
    squares_sems,
    back_sems,
    column_sems,
    part_sems,
    compressed_sems,
    embed_sems,
    local_sem,
):
    reps, owners, units, rows, cap, cols = dims
    lanes = reps * cols
    quads = rows // reps
    real = units * quads
    sent = share_send.shape[1]
    padded = summed.shape[0]
    block = quads * cap
    sources = owners * quads
    me_rep = lax.axis_index("rep")
    me_own = lax.axis_index("own")

    def rep_peer(step):
        return lax.rem(me_rep + step, reps)

    def rep_source(step):
        return lax.rem(me_rep + reps - step, reps)

    def own_peer(step):
        return lax.rem(me_own + step, owners)

    def own_source(step):
        return lax.rem(me_own + owners - step, owners)

    def rep_copy(src, dst, sems, step):
        return pltpu.make_async_remote_copy(
            src_ref=src,
            dst_ref=dst,
            send_sem=sems.at[0, step - 1],
            recv_sem=sems.at[1, step - 1],
            device_id=(rep_peer(step), me_own),
            device_id_type=MESH,
        )

    def own_copy(src, dst, sems, step):
        return pltpu.make_async_remote_copy(
            src_ref=src,
            dst_ref=dst,
            send_sem=sems.at[0, step - 1],
            recv_sem=sems.at[1, step - 1],
            device_id=(me_rep, own_peer(step)),
            device_id_type=MESH,
        )

    def loop(count, body):
        def run(step, carry):
            body(step)
            return carry

        lax.fori_loop(0, count, run, 0)

    def rep_loop(body):
        loop(reps - 1, lambda step: body(step + 1))

    def own_loop(body):
        loop(owners - 1, lambda step: body(step + 1))

    def aligned(start, size, by):
        return pl.ds(pl.multiple_of(start, by), size)

    barrier = pltpu.get_barrier_semaphore()
    rep_loop(
        lambda step: pl.semaphore_signal(
            barrier, inc=1, device_id=(rep_peer(step), me_own), device_id_type=MESH
        )
    )
    own_loop(
        lambda step: pl.semaphore_signal(
            barrier, inc=1, device_id=(me_rep, own_peer(step)), device_id_type=MESH
        )
    )

    anchor_embed = anchor_embed_ref[...]
    my_projection = projection_ref[:, aligned(me_rep * lanes, lanes, lanes)].astype(F32)
    last = (((1,), (1,)), ((), ()))
    part = lax.dot_general(my_projection, anchor_embed, last, precision=HIGHEST, preferred_element_type=F32)
    part_send[...] = part - lax.dot_general(
        projection_ref[...], embed_ref[...], last, preferred_element_type=F32
    ) / reps
    pl.semaphore_wait(barrier, reps - 1 + owners - 1)

    ranks = part_send.shape[0] // reps

    def part_copy(step):
        return rep_copy(
            part_send.at[aligned(rep_peer(step) * ranks, ranks, 8)], part_recv.at[step - 1], part_sems, step
        )

    rep_loop(lambda step: part_copy(step).start())

    row_count = dense_ref.shape[0]
    stored[pl.ds(0, row_count), :] = dense_ref[...].astype(F32)
    stored[pl.ds(row_count, padded * reps - row_count), :] = jnp.zeros(
        (padded * reps - row_count, lanes), F32
    )
    for group in range(reps):
        wide[:, group * lanes : (group + 1) * lanes] = stored[
            pl.ds(group, padded, stride=reps), :
        ].astype(BF16)

    def swap_pick(which):
        at = iota((reps * lanes, lanes), 0)
        lane = iota((reps * lanes, lanes), 1)
        return onehot(((at // lanes) * cols + at % cols == lane) & ((at // cols) % reps == which))

    def share_of(which):
        return jnp.dot(wide[...], swap_pick(which), preferred_element_type=F32)

    def share_copy(step):
        return rep_copy(share_send.at[step - 1], share_recv.at[step - 1], share_sems, step)

    def send_share(step):
        share_send[step - 1] = share_of(rep_peer(step))[:sent].astype(BF16)
        share_copy(step).start()

    rep_loop(send_share)
    summed_own = share_of(me_rep)[:sent]

    owner_row = owner_row_ref[...]
    owner_col = owner_col_ref[...]

    def targets(owner_at, owner_over, at_axis):
        shape = (padded, padded)
        at = iota(shape, at_axis)
        over = iota(shape, 1 - at_axis)
        before = (owner_at == owner_over) & (over < at) & (over % quads == at % quads)
        rank = jnp.sum(jnp.where(before, 1.0, 0.0), axis=1 - at_axis, keepdims=True).astype(jnp.int32)
        short = (1, padded) if at_axis == 1 else (padded, 1)
        quad = iota(short, at_axis)
        target = owner_at * block + (quad % quads) * cap + rank
        return jnp.where(quad < real, target, -1)

    row_targets = targets(owner_row, owner_col, 1)
    col_targets = targets(owner_col, owner_row, 0)
    slot_rows = slot_pick.shape[0]
    slot_pick[...] = onehot(iota((slot_rows, padded), 0) == row_targets)
    unit_pick[...] = onehot(iota((padded, slot_rows), 1) == col_targets)
    held = jnp.sum(
        jnp.where((owner_row == me_own) & (iota((1, padded), 1) < real), 1.0, 0.0), axis=1, keepdims=True
    )
    width = sources * reps
    at = iota((width, width), 0)
    to = iota((width, width), 1)
    to_rows[...] = onehot((at % sources) * reps + at // sources == to)
    from_rows[...] = onehot((at % reps) * sources + at // reps == to)

    my_ranks = aligned(me_rep * ranks, ranks, 8)
    rep_loop(lambda step: part_copy(step).wait_recv())
    total = part_send[my_ranks, :]
    for step in range(1, reps):
        total = total + part_recv[step - 1]
    part_sum[...] = total
    compressed[my_ranks, :] = total

    def compressed_copy(step, source):
        return rep_copy(part_sum, compressed.at[aligned(source * ranks, ranks, 8)], compressed_sems, step)

    rep_loop(lambda step: compressed_copy(step, me_rep).start())

    rep_loop(lambda step: share_copy(step).wait_recv())
    share_total = summed_own
    for step in range(1, reps):
        share_total = share_total + share_recv[step - 1].astype(F32)
    summed[pl.ds(0, sent), :] = share_total.astype(BF16)
    summed[pl.ds(sent, padded - sent), :] = jnp.zeros((padded - sent, lanes), BF16)
    packed = jnp.dot(slot_pick[...], summed[...], preferred_element_type=F32).astype(BF16)
    out_send[...] = packed

    def own_block(index):
        return aligned(index * block, block, 16)

    def out_copy(step, source):
        return own_copy(
            out_send.at[own_block(own_peer(step))], out_recv.at[own_block(source)], out_sems, step
        )

    own_loop(lambda step: out_copy(step, me_own).start())
    out_recv[own_block(me_own), :] = out_send[own_block(me_own), :]

    rep_loop(lambda step: compressed_copy(step, rep_source(step)).wait_recv())
    change_embed = compressed[...]
    moment_embed_new = OUTER_MOMENTUM * moment_embed_ref[...] + change_embed
    moment_embed_out[...] = moment_embed_new
    first = (((0,), (0,)), ((), ()))
    anchor_embed_new = anchor_embed_ref[...] - OUTER_RATE * lax.dot_general(
        change_embed + OUTER_MOMENTUM * moment_embed_new,
        my_projection,
        first,
        precision=HIGHEST,
        preferred_element_type=F32,
    )
    anchor_embed_out[...] = anchor_embed_new
    embed_send[...] = anchor_embed_new.astype(BF16)

    def embed_copy(step, source):
        return rep_copy(embed_send, embed_out.at[:, aligned(source * lanes, lanes, lanes)], embed_sems, step)

    half = reps // 2
    loop(half, lambda step: embed_copy(step + 1, me_rep).start())
    own_embed = pltpu.make_async_copy(
        embed_send, embed_out.at[:, aligned(me_rep * lanes, lanes, lanes)], local_sem
    )
    own_embed.start()

    own_loop(lambda step: out_copy(step, own_source(step)).wait_recv())
    slots_f32[...] = out_recv[...].astype(F32)
    for slot in range(cap):
        turned = slots_f32[pl.ds(slot, sources, stride=cap), :].T
        for group in range(reps):
            spread[slot * cols : (slot + 1) * cols, group * sources : (group + 1) * sources] = turned[
                group * cols : (group + 1) * cols
            ].astype(BF16)
    owned = jnp.dot(spread[...], to_rows[...], preferred_element_type=F32)
    change[...] = anchor_ref[...] - owned / reps
    squares_send[...] = jnp.zeros_like(squares_send)
    for slot in range(cap):
        one = change[slot * cols : (slot + 1) * cols, :]
        total = jnp.sum(jnp.sum(one * one, axis=0, keepdims=True), axis=1, keepdims=True)
        squares_send[slot : slot + 1, :] = jnp.broadcast_to(total, (1, squares_send.shape[1]))

    def squares_copy(step):
        return rep_copy(squares_send, squares_recv.at[step - 1], squares_sems, step)

    rep_loop(lambda step: squares_copy(step).start())
    loop(reps - 1 - half, lambda step: embed_copy(step + 1 + half, me_rep).start())
    rep_loop(lambda step: squares_copy(step).wait_recv())
    squares = squares_send[...]
    for step in range(1, reps):
        squares = squares + squares_recv[step - 1]
    root_mean = jnp.sqrt(squares / (owners * rows * lanes) + EPSILON)
    factors = jnp.minimum(1.0, CLIP_RMS / root_mean)
    for slot in range(cap):
        at = pl.ds(slot * cols, cols)
        live = jnp.where(held > slot * quads, 1.0, 0.0)
        clipped = change[at, :] * factors[slot : slot + 1, 0:1]
        moment_new = live * (OUTER_MOMENTUM * moment_ref[at, :] + clipped)
        anchor_new = live * (anchor_ref[at, :] - OUTER_RATE * (clipped + OUTER_MOMENTUM * moment_new))
        moment_out[at, :] = moment_new
        anchor_out[at, :] = anchor_new
        spread[at, :] = anchor_new.astype(BF16)
    regrouped = jnp.dot(spread[...], from_rows[...], preferred_element_type=F32)
    for slot in range(cap):
        turned = jnp.concatenate(
            [
                regrouped[slot * cols : (slot + 1) * cols, group * sources : (group + 1) * sources]
                for group in range(reps)
            ],
            axis=0,
        ).T
        slots_f32[pl.ds(slot, sources, stride=cap), :] = turned
    back_send[...] = slots_f32[...].astype(BF16)

    def back_copy(step, source):
        return own_copy(
            back_send.at[own_block(own_peer(step))], back_recv.at[own_block(source)], back_sems, step
        )

    own_loop(lambda step: back_copy(step, me_own).start())
    back_recv[own_block(me_own), :] = back_send[own_block(me_own), :]
    own_loop(lambda step: back_copy(step, own_source(step)).wait_recv())

    column_send[...] = jnp.dot(unit_pick[...], back_recv[...], preferred_element_type=F32)[:sent].astype(BF16)

    def column_copy(step, source):
        return rep_copy(column_send, column_recv.at[source], column_sems, step)

    rep_loop(lambda step: column_copy(step, me_rep).start())
    column_recv[me_rep] = column_send[...]
    rep_loop(lambda step: column_copy(step, rep_source(step)).wait_recv())
    gathered = jnp.concatenate([column_recv[group] for group in range(reps)], axis=1)
    for group in range(reps):
        stored[pl.ds(group, sent, stride=reps), :] = jnp.dot(
            gathered, swap_pick(group), preferred_element_type=F32
        )
    dense_out[...] = stored[pl.ds(0, row_count), :].astype(BF16)

    rep_loop(lambda step: embed_copy(step, rep_source(step)).wait_recv())
    own_embed.wait()
    rep_loop(lambda step: part_copy(step).wait_send())
    rep_loop(lambda step: share_copy(step).wait_send())
    rep_loop(lambda step: compressed_copy(step, me_rep).wait_send())
    rep_loop(lambda step: squares_copy(step).wait_send())
    rep_loop(lambda step: embed_copy(step, me_rep).wait_send())
    rep_loop(lambda step: column_copy(step, me_rep).wait_send())
    own_loop(lambda step: out_copy(step, me_own).wait_send())
    own_loop(lambda step: back_copy(step, me_own).wait_send())


def round_up(value, to):
    return -(-value // to) * to


def on_device(
    local_dense,
    owner_list,
    anchor_slots,
    moment_slots,
    local_embed,
    anchor_embed,
    moment_embed,
    projection,
):
    owners = lax.axis_size("own")
    reps = lax.axis_size("rep")
    _, rows, units, lanes = local_dense.shape
    _, width, cap, cols = anchor_slots.shape
    vocab, rank = moment_embed.shape
    features = projection.shape[0]
    quads = rows // reps
    real = units * quads
    sent = round_up(real, 16)
    padded = round_up(real, 128)
    block = quads * cap
    slot_rows = owners * block

    def turn_slots(slots):
        return jnp.transpose(slots[0], (1, 2, 0)).reshape(cap * cols, width)

    def unturn_slots(slots):
        return jnp.transpose(slots.reshape(cap, cols, width), (2, 0, 1))[None]

    owner_quads = jnp.pad(jnp.repeat(owner_list, quads), (0, padded - real))
    vmem = pl.BlockSpec(memory_space=pltpu.VMEM)
    rep_sems = pltpu.SemaphoreType.DMA((2, reps - 1))
    own_sems = pltpu.SemaphoreType.DMA((2, owners - 1))
    dense, anchor_new, moment_new, embed_weights, anchor_embed_new, moment_embed_new = pl.pallas_call(
        functools.partial(kernel, (reps, owners, units, rows, cap, cols)),
        out_shape=(
            jax.ShapeDtypeStruct((units * rows, lanes), BF16),
            jax.ShapeDtypeStruct((cap * cols, width), F32),
            jax.ShapeDtypeStruct((cap * cols, width), F32),
            jax.ShapeDtypeStruct((vocab, features), BF16),
            jax.ShapeDtypeStruct((vocab, lanes), F32),
            jax.ShapeDtypeStruct((rank, vocab), F32),
        ),
        in_specs=[vmem] * 9,
        out_specs=(vmem, vmem, vmem, pl.BlockSpec(memory_space=pl.ANY), vmem, vmem),
        scratch_shapes=[
            pltpu.VMEM((padded * reps, lanes), F32),
            pltpu.VMEM((padded, reps * lanes), BF16),
            pltpu.VMEM((reps - 1, sent, lanes), BF16),
            pltpu.VMEM((reps - 1, sent, lanes), BF16),
            pltpu.VMEM((padded, lanes), BF16),
            pltpu.VMEM((slot_rows, padded), BF16),
            pltpu.VMEM((padded, slot_rows), BF16),
            pltpu.VMEM((width, width), BF16),
            pltpu.VMEM((width, width), BF16),
            pltpu.VMEM((slot_rows, lanes), BF16),
            pltpu.VMEM((slot_rows, lanes), BF16),
            pltpu.VMEM((slot_rows, lanes), F32),
            pltpu.VMEM((cap * cols, width), BF16),
            pltpu.VMEM((cap * cols, width), F32),
            pltpu.VMEM((round_up(cap, 8), lanes), F32),
            pltpu.VMEM((reps - 1, round_up(cap, 8), lanes), F32),
            pltpu.VMEM((slot_rows, lanes), BF16),
            pltpu.VMEM((slot_rows, lanes), BF16),
            pltpu.VMEM((sent, lanes), BF16),
            pltpu.VMEM((reps, sent, lanes), BF16),
            pltpu.VMEM((rank, vocab), F32),
            pltpu.VMEM((reps - 1, rank // reps, vocab), F32),
            pltpu.VMEM((rank // reps, vocab), F32),
            pltpu.VMEM((rank, vocab), F32),
            pltpu.VMEM((vocab, lanes), BF16),
            rep_sems,
            own_sems,
            rep_sems,
            own_sems,
            rep_sems,
            rep_sems,
            rep_sems,
            rep_sems,
            pltpu.SemaphoreType.DMA,
        ],
        compiler_params=pltpu.CompilerParams(
            collective_id=0, has_side_effects=True, vmem_limit_bytes=62 * 1024 * 1024
        ),
        name="outer_step",
    )(
        jnp.transpose(local_dense[0], (1, 0, 2)).reshape(units * rows, lanes),
        owner_quads[None, :],
        owner_quads[:, None],
        turn_slots(anchor_slots),
        turn_slots(moment_slots),
        local_embed[0],
        anchor_embed,
        moment_embed.T,
        projection.T,
    )
    return (
        jnp.transpose(dense.reshape(units, rows, lanes), (1, 0, 2)),
        unturn_slots(anchor_new),
        unturn_slots(moment_new),
        embed_weights,
        anchor_embed_new,
        moment_embed_new.T,
    )


def solution(mesh):
    placed = (
        P("rep", "own", None, None),
        P(),
        P("own", None, None, "rep"),
        P("own", None, None, "rep"),
        P("rep", "own", None),
        P("own", "rep"),
        P("own", None),
        P(),
    )
    return jax.shard_map(
        on_device,
        mesh=mesh,
        in_specs=placed,
        out_specs=(
            P("own", None, None),
            P("own", None, None, "rep"),
            P("own", None, None, "rep"),
            P("own", None),
            P("own", "rep"),
            P("own", None),
        ),
        check_vma=False,
    )
```

```python
import functools

import jax
import jax.numpy as jnp
from jax import lax
from jax.experimental import pallas as pl
from jax.experimental.pallas import tpu as pltpu
from jax.sharding import PartitionSpec as P

OUTER_MOMENTUM = 0.9
OUTER_RATE = 0.7
CLIP_RMS = 2.0
EPSILON = 1e-06
MESH = pl.DeviceIdType.MESH
F32 = jnp.float32
BF16 = jnp.bfloat16
HIGHEST = lax.Precision.HIGHEST


def iota(shape, axis):
    return lax.broadcasted_iota(jnp.int32, shape, axis)


def onehot(condition):
    return jnp.where(condition, 1.0, 0.0).astype(BF16)


def swap_matrix(reps, cols):
    lanes = reps * cols
    at = iota((reps * lanes, 1), 0)
    to = ((at // cols) % reps) * lanes + (at // lanes) * cols + at % cols
    return onehot(iota((reps * lanes, reps * lanes), 1) == to)


def kernel(
    dims,
    owner_ref,
    dense_hbm,
    embed_hbm,
    anchor_embed_hbm,
    projection_hbm,
    moment_embed_hbm,
    anchor_hbm,
    moment_hbm,
    column_out,
    embed_out,
    anchor_out,
    moment_out,
    anchor_embed_out,
    moment_embed_out,
    dense_ref,
    embed_ref,
    anchor_embed_ref,
    projection_ref,
    moment_embed_ref,
    anchor_ref,
    moment_ref,
    anchor_new_ref,
    moment_new_ref,
    anchor_embed_new_ref,
    moment_embed_new_ref,
    swap,
    stored,
    wide,
    share_send,
    share_recv,
    summed,
    slot_pick,
    unit_pick,
    to_rows,
    from_rows,
    out_send,
    out_recv,
    slots_f32,
    spread,
    change,
    squares_send,
    squares_recv,
    back_send,
    back_recv,
    column_send,
    part_send,
    part_recv,
    part_sum,
    compressed,
    embed_send,
    share_sems,
    out_sems,
    squares_sems,
    back_sems,
    part_sems,
    compressed_sems,
    column_sems,
    embed_sems,
    in_sems,
    local_sems,
):
    reps, owners, units, rows, cap, cols = dims
    lanes = reps * cols
    quads = rows // reps
    real = units * quads
    sent = share_send.shape[1]
    padded = summed.shape[0]
    block = quads * cap
    sources = owners * quads
    ring = reps // 2
    me_rep = lax.axis_index("rep")
    me_own = lax.axis_index("own")
    side = me_rep // ring
    place = lax.rem(me_rep, ring)

    def rep_at(flip, move):
        return lax.rem(side + flip, 2) * ring + lax.rem(place + move, ring)

    def rep_peer(step):
        return rep_at(step // ring, lax.rem(step, ring))

    def rep_source(step):
        return rep_at(step // ring, ring - lax.rem(step, ring))

    def own_peer(step):
        return lax.rem(me_own + step, owners)

    def own_source(step):
        return lax.rem(me_own + owners - step, owners)

    def send(src, dst, sems, index, device):
        return pltpu.make_async_remote_copy(
            src_ref=src,
            dst_ref=dst,
            send_sem=sems.at[0, index],
            recv_sem=sems.at[1, index],
            device_id=device,
            device_id_type=MESH,
        )

    def rep_copy(src, dst, sems, step):
        return send(src, dst, sems, step - 1, (rep_peer(step), me_own))

    def own_copy(src, dst, sems, step):
        return send(src, dst, sems, step - 1, (me_rep, own_peer(step)))

    def loop(count, body):
        def run(step, carry):
            body(step)
            return carry

        lax.fori_loop(0, count, run, 0)

    def rep_loop(body):
        loop(reps - 1, lambda step: body(step + 1))

    def own_loop(body):
        loop(owners - 1, lambda step: body(step + 1))

    def aligned(start, size, by):
        return pl.ds(pl.multiple_of(start, by), size)

    class Spread:
        def __init__(self, own, slots, sems):
            half = slots.shape[1] // 2 // 16 * 16
            first = pl.ds(0, half)
            second = pl.ds(half, slots.shape[1] - half)
            up, down, over = rep_at(0, 1), rep_at(0, ring - 1), rep_at(1, 0)
            over_up, over_down = rep_at(1, 1), rep_at(1, ring - 1)
            far, over_far = rep_at(0, 2), rep_at(1, 2)
            self.own_slot = slots.at[me_rep]
            self.own = own
            self.sems = sems
            self.sends = [
                (own, slots.at[me_rep], over),
                (own, slots.at[me_rep], up),
                (own, slots.at[me_rep], down),
                (slots.at[over], slots.at[over], up),
                (slots.at[over], slots.at[over], down),
                (slots.at[down, first], slots.at[down, first], up),
                (slots.at[up, second], slots.at[up, second], down),
                (slots.at[over_down, first], slots.at[over_down, first], up),
                (slots.at[over_up, second], slots.at[over_up, second], down),
            ]
            self.lands = [
                slots.at[over],
                slots.at[down],
                slots.at[up],
                slots.at[over_down],
                slots.at[over_up],
                slots.at[far, first],
                slots.at[far, second],
                slots.at[over_far, first],
                slots.at[over_far, second],
            ]

        def copy(self, index):
            src, dst, device = self.sends[index]
            return send(src, dst, self.sems, index, (device, me_own))

        def start(self, *indices):
            for index in indices:
                self.copy(index).start()

        def arrived(self, *indices):
            for index in indices:
                land = self.lands[index]
                send(land, land, self.sems, index, (rep_at(1, 0), me_own)).wait_recv()

        def finish(self):
            for index in range(len(self.sends)):
                self.copy(index).wait_send()

    def fetch(index, src, dst):
        return pltpu.make_async_copy(src, dst, in_sems.at[index])

    fetches = [
        fetch(0, dense_hbm, dense_ref),
        fetch(1, embed_hbm, embed_ref),
        fetch(2, anchor_embed_hbm, anchor_embed_ref),
        fetch(3, projection_hbm, projection_ref),
        fetch(4, moment_embed_hbm, moment_embed_ref),
        fetch(5, anchor_hbm, anchor_ref),
        fetch(6, moment_hbm, moment_ref),
    ]
    for one in fetches:
        one.start()

    barrier = pltpu.get_barrier_semaphore()
    rep_loop(
        lambda step: pl.semaphore_signal(
            barrier, inc=1, device_id=(rep_peer(step), me_own), device_id_type=MESH
        )
    )
    own_loop(
        lambda step: pl.semaphore_signal(
            barrier, inc=1, device_id=(me_rep, own_peer(step)), device_id_type=MESH
        )
    )

    swap[...] = swap_matrix(reps, cols)
    row_count = dense_ref.shape[0]
    fetches[0].wait()
    stored[pl.ds(0, row_count), :] = dense_ref[...].astype(F32)
    stored[pl.ds(row_count, padded * reps - row_count), :] = jnp.zeros(
        (padded * reps - row_count, lanes), F32
    )
    for group in range(reps):
        wide[:, group * lanes : (group + 1) * lanes] = stored[
            pl.ds(group, padded, stride=reps), :
        ].astype(BF16)

    def share_of(which):
        return jnp.dot(
            wide[...], swap[:, aligned(which * lanes, lanes, lanes)], preferred_element_type=F32
        )[:sent]

    def share_copy(step):
        return rep_copy(share_send.at[step - 1], share_recv.at[step - 1], share_sems, step)

    order = sorted(range(1, reps), key=lambda step: (step == ring, abs(step % ring - ring // 2)))
    for count, step in enumerate(order):
        share_send[step - 1] = share_of(rep_peer(step)).astype(BF16)
        if count == 0:
            pl.semaphore_wait(barrier, reps - 1 + owners - 1)
        share_copy(step).start()
    summed_own = share_of(me_rep)

    for one in fetches[1:]:
        one.wait()
    my_projection = projection_ref[:, aligned(me_rep * lanes, lanes, lanes)].astype(F32)
    last = (((1,), (1,)), ((), ()))
    part = lax.dot_general(
        my_projection, anchor_embed_ref[...], last, precision=HIGHEST, preferred_element_type=F32
    )
    part_send[...] = part - lax.dot_general(
        projection_ref[...], embed_ref[...], last, preferred_element_type=F32
    ) / reps
    ranks = part_send.shape[0] // reps

    def part_copy(step):
        return rep_copy(
            part_send.at[aligned(rep_peer(step) * ranks, ranks, 8)], part_recv.at[step - 1], part_sems, step
        )

    rep_loop(lambda step: part_copy(step).start())

    owners_of = owner_ref[...].astype(F32)
    expand = onehot(iota((units, padded), 0) == iota((units, padded), 1) // quads)
    owner_row = jnp.dot(
        jnp.broadcast_to(owners_of, (8, units)).astype(BF16), expand, preferred_element_type=F32
    )[0:1].astype(jnp.int32)
    owner_col = jnp.sum(
        jnp.where(iota((padded, units), 1) == iota((padded, units), 0) // quads, owners_of, 0.0),
        axis=1,
        keepdims=True,
    ).astype(jnp.int32)

    def targets(owner_at, owner_over, at_axis):
        shape = (padded, padded)
        at = iota(shape, at_axis)
        over = iota(shape, 1 - at_axis)
        before = (owner_at == owner_over) & (over < at) & (over % quads == at % quads)
        rank = jnp.sum(jnp.where(before, 1.0, 0.0), axis=1 - at_axis, keepdims=True).astype(jnp.int32)
        short = (1, padded) if at_axis == 1 else (padded, 1)
        quad = iota(short, at_axis)
        target = owner_at * block + (quad % quads) * cap + rank
        return jnp.where(quad < real, target, -1)

    row_targets = targets(owner_row, owner_col, 1)
    col_targets = targets(owner_col, owner_row, 0)
    slot_rows = slot_pick.shape[0]
    slot_pick[...] = onehot(iota((slot_rows, padded), 0) == row_targets)
    unit_pick[...] = onehot(iota((padded, slot_rows), 1) == col_targets)
    held = jnp.sum(
        jnp.where((owner_row == me_own) & (iota((1, padded), 1) < real), 1.0, 0.0), axis=1, keepdims=True
    )
    width = sources * reps
    at = iota((width, 1), 0)
    to = iota((width, width), 1)
    to_rows[...] = onehot((at % sources) * reps + at // sources == to)
    from_rows[...] = onehot((at % reps) * sources + at // reps == to)

    rep_loop(lambda step: share_copy(step).wait_recv())
    share_total = summed_own
    for step in range(1, reps):
        share_total = share_total + share_recv[step - 1].astype(F32)
    summed[pl.ds(0, sent), :] = share_total.astype(BF16)
    summed[pl.ds(sent, padded - sent), :] = jnp.zeros((padded - sent, lanes), BF16)
    out_send[...] = jnp.dot(slot_pick[...], summed[...], preferred_element_type=F32).astype(BF16)

    def own_block(index):
        return aligned(index * block, block, 16)

    def out_copy(step, source):
        return own_copy(
            out_send.at[own_block(own_peer(step))], out_recv.at[own_block(source)], out_sems, step
        )

    own_loop(lambda step: out_copy(step, me_own).start())
    out_recv[own_block(me_own), :] = out_send[own_block(me_own), :]

    my_ranks = aligned(me_rep * ranks, ranks, 8)
    rep_loop(lambda step: part_copy(step).wait_recv())
    total = part_send[my_ranks, :]
    for step in range(1, reps):
        total = total + part_recv[step - 1]
    part_sum[...] = total
    compressed[my_ranks, :] = total

    def compressed_copy(step, source):
        return rep_copy(part_sum, compressed.at[aligned(source * ranks, ranks, 8)], compressed_sems, step)

    rep_loop(lambda step: compressed_copy(step, me_rep).start())
    rep_loop(lambda step: compressed_copy(step, rep_source(step)).wait_recv())
    change_embed = compressed[...]
    moment_embed_new = OUTER_MOMENTUM * moment_embed_ref[...] + change_embed
    moment_embed_new_ref[...] = moment_embed_new
    first = (((0,), (0,)), ((), ()))
    anchor_embed_new = anchor_embed_ref[...] - OUTER_RATE * lax.dot_general(
        change_embed + OUTER_MOMENTUM * moment_embed_new,
        my_projection,
        first,
        precision=HIGHEST,
        preferred_element_type=F32,
    )
    anchor_embed_new_ref[...] = anchor_embed_new
    embed_send[...] = anchor_embed_new.astype(BF16)
    embed_spread = Spread(embed_send, embed_out, embed_sems)
    embed_spread.start(0, 1, 2)

    def store(index, src, dst):
        return pltpu.make_async_copy(src, dst, local_sems.at[index])

    stores = [
        store(0, embed_send, embed_spread.own_slot),
        store(1, anchor_embed_new_ref, anchor_embed_out),
        store(2, moment_embed_new_ref, moment_embed_out),
    ]
    for one in stores:
        one.start()

    own_loop(lambda step: out_copy(step, own_source(step)).wait_recv())
    slots_f32[...] = out_recv[...].astype(F32)
    for slot in range(cap):
        turned = slots_f32[pl.ds(slot, sources, stride=cap), :].T
        for group in range(reps):
            spread[slot * cols : (slot + 1) * cols, group * sources : (group + 1) * sources] = turned[
                group * cols : (group + 1) * cols
            ].astype(BF16)
    owned = jnp.dot(spread[...], to_rows[...], preferred_element_type=F32)
    change[...] = anchor_ref[...] - owned / reps
    squares_send[...] = jnp.zeros_like(squares_send)
    for slot in range(cap):
        one = change[slot * cols : (slot + 1) * cols, :]
        total = jnp.sum(jnp.sum(one * one, axis=0, keepdims=True), axis=1, keepdims=True)
        squares_send[slot : slot + 1, :] = jnp.broadcast_to(total, (1, squares_send.shape[1]))

    def squares_copy(step):
        return rep_copy(squares_send, squares_recv.at[step - 1], squares_sems, step)

    rep_loop(lambda step: squares_copy(step).start())
    embed_spread.arrived(0, 1, 2)
    embed_spread.start(3, 4, 5, 6)
    rep_loop(lambda step: squares_copy(step).wait_recv())
    squares = squares_send[...]
    for step in range(1, reps):
        squares = squares + squares_recv[step - 1]
    root_mean = jnp.sqrt(squares / (owners * rows * lanes) + EPSILON)
    factors = jnp.minimum(1.0, CLIP_RMS / root_mean)
    for slot in range(cap):
        at = pl.ds(slot * cols, cols)
        live = jnp.where(held > slot * quads, 1.0, 0.0)
        clipped = change[at, :] * factors[slot : slot + 1, 0:1]
        moment_new = live * (OUTER_MOMENTUM * moment_ref[at, :] + clipped)
        anchor_new = live * (anchor_ref[at, :] - OUTER_RATE * (clipped + OUTER_MOMENTUM * moment_new))
        moment_new_ref[at, :] = moment_new
        anchor_new_ref[at, :] = anchor_new
        spread[at, :] = anchor_new.astype(BF16)
    regrouped = jnp.dot(spread[...], from_rows[...], preferred_element_type=F32)
    for slot in range(cap):
        turned = jnp.concatenate(
            [
                regrouped[slot * cols : (slot + 1) * cols, group * sources : (group + 1) * sources]
                for group in range(reps)
            ],
            axis=0,
        ).T
        slots_f32[pl.ds(slot, sources, stride=cap), :] = turned
    back_send[...] = slots_f32[...].astype(BF16)

    def back_copy(step, source):
        return own_copy(
            back_send.at[own_block(own_peer(step))], back_recv.at[own_block(source)], back_sems, step
        )

    own_loop(lambda step: back_copy(step, me_own).start())
    back_recv[own_block(me_own), :] = back_send[own_block(me_own), :]
    late = [store(3, anchor_new_ref, anchor_out), store(4, moment_new_ref, moment_out)]
    for one in late:
        one.start()
    embed_spread.arrived(3, 4)
    embed_spread.start(7, 8)
    own_loop(lambda step: back_copy(step, own_source(step)).wait_recv())

    column_send[...] = jnp.dot(unit_pick[...], back_recv[...], preferred_element_type=F32)[:sent].astype(BF16)
    column_spread = Spread(column_send, column_out, column_sems)
    column_spread.start(0, 1, 2)
    late.append(store(5, column_send, column_spread.own_slot))
    late[-1].start()
    column_spread.arrived(0)
    column_spread.start(3, 4)
    column_spread.arrived(1)
    column_spread.start(5)
    column_spread.arrived(2)
    column_spread.start(6)
    column_spread.arrived(3)
    column_spread.start(7)
    column_spread.arrived(4)
    column_spread.start(8)

    for one in stores + late:
        one.wait()
    embed_spread.arrived(5, 6, 7, 8)
    embed_spread.finish()
    rep_loop(lambda step: part_copy(step).wait_send())
    rep_loop(lambda step: share_copy(step).wait_send())
    rep_loop(lambda step: compressed_copy(step, me_rep).wait_send())
    rep_loop(lambda step: squares_copy(step).wait_send())
    own_loop(lambda step: out_copy(step, me_own).wait_send())
    own_loop(lambda step: back_copy(step, me_own).wait_send())
    column_spread.arrived(5, 6, 7, 8)
    column_spread.finish()


def finish_kernel(
    cols,
    column_ref,
    embed_ref,
    anchor_ref,
    moment_ref,
    anchor_embed_ref,
    moment_embed_ref,
    dense_out,
    embed_out,
    anchor_out,
    moment_out,
    anchor_embed_out,
    moment_embed_out,
    swap,
    stored,
):
    reps, size, lanes = column_ref.shape

    @pl.when(pl.program_id(0) == 0)
    def _():
        swap[...] = swap_matrix(reps, cols)

    gathered = jnp.concatenate([column_ref[group] for group in range(reps)], axis=1)
    ordered = jnp.dot(gathered, swap[...], preferred_element_type=F32)
    for group in range(reps):
        stored[pl.ds(group, size, stride=reps), :] = ordered[:, group * lanes : (group + 1) * lanes]
    dense_out[...] = stored[...].astype(BF16)
    for group in range(reps):
        embed_out[:, group * lanes : (group + 1) * lanes] = embed_ref[group]
    anchor_out[...] = anchor_ref[...]
    moment_out[...] = moment_ref[...]
    anchor_embed_out[...] = anchor_embed_ref[...]
    moment_embed_out[...] = moment_embed_ref[...]


def round_up(value, to):
    return -(-value // to) * to


def on_device(
    local_dense,
    owner_list,
    anchor_slots,
    moment_slots,
    local_embed,
    anchor_embed,
    moment_embed,
    projection,
):
    owners = lax.axis_size("own")
    reps = lax.axis_size("rep")
    _, rows, units, lanes = local_dense.shape
    _, width, cap, cols = anchor_slots.shape
    vocab, rank = moment_embed.shape
    features = projection.shape[0]
    quads = rows // reps
    real = units * quads
    sent = round_up(real, 16)
    padded = round_up(real, 128)
    block = quads * cap
    slot_rows = owners * block
    slot_cols = cap * cols
    steps = 4

    def turn_slots(slots):
        return jnp.transpose(slots[0], (1, 2, 0)).reshape(slot_cols, width)

    def unturn_slots(slots):
        return jnp.transpose(slots.reshape(cap, cols, width), (2, 0, 1))[None]

    vmem = pl.BlockSpec(memory_space=pltpu.VMEM)
    anywhere = pl.BlockSpec(memory_space=pl.ANY)
    rep_sems = pltpu.SemaphoreType.DMA((2, reps - 1))
    own_sems = pltpu.SemaphoreType.DMA((2, owners - 1))
    spread_sems = pltpu.SemaphoreType.DMA((2, 9))
    slot_shape = pltpu.VMEM((slot_cols, width), F32)
    column, embed_new, *rest = pl.pallas_call(
        functools.partial(kernel, (reps, owners, units, rows, cap, cols)),
        out_shape=(
            jax.ShapeDtypeStruct((reps, sent, lanes), BF16),
            jax.ShapeDtypeStruct((reps, vocab, lanes), BF16),
            jax.ShapeDtypeStruct((slot_cols, width), F32),
            jax.ShapeDtypeStruct((slot_cols, width), F32),
            jax.ShapeDtypeStruct((vocab, lanes), F32),
            jax.ShapeDtypeStruct((rank, vocab), F32),
        ),
        in_specs=[vmem] + [anywhere] * 7,
        out_specs=(anywhere,) * 6,
        scratch_shapes=[
            pltpu.VMEM((units * rows, lanes), BF16),
            pltpu.VMEM((vocab, features), BF16),
            pltpu.VMEM((vocab, lanes), F32),
            pltpu.VMEM((rank, features), BF16),
            pltpu.VMEM((rank, vocab), F32),
            slot_shape,
            slot_shape,
            slot_shape,
            slot_shape,
            pltpu.VMEM((vocab, lanes), F32),
            pltpu.VMEM((rank, vocab), F32),
            pltpu.VMEM((reps * lanes, reps * lanes), BF16),
            pltpu.VMEM((padded * reps, lanes), F32),
            pltpu.VMEM((padded, reps * lanes), BF16),
            pltpu.VMEM((reps - 1, sent, lanes), BF16),
            pltpu.VMEM((reps - 1, sent, lanes), BF16),
            pltpu.VMEM((padded, lanes), BF16),
            pltpu.VMEM((slot_rows, padded), BF16),
            pltpu.VMEM((padded, slot_rows), BF16),
            pltpu.VMEM((width, width), BF16),
            pltpu.VMEM((width, width), BF16),
            pltpu.VMEM((slot_rows, lanes), BF16),
            pltpu.VMEM((slot_rows, lanes), BF16),
            pltpu.VMEM((slot_rows, lanes), F32),
            pltpu.VMEM((slot_cols, width), BF16),
            slot_shape,
            pltpu.VMEM((round_up(cap, 8), lanes), F32),
            pltpu.VMEM((reps - 1, round_up(cap, 8), lanes), F32),
            pltpu.VMEM((slot_rows, lanes), BF16),
            pltpu.VMEM((slot_rows, lanes), BF16),
            pltpu.VMEM((sent, lanes), BF16),
            pltpu.VMEM((rank, vocab), F32),
            pltpu.VMEM((reps - 1, rank // reps, vocab), F32),
            pltpu.VMEM((rank // reps, vocab), F32),
            pltpu.VMEM((rank, vocab), F32),
            pltpu.VMEM((vocab, lanes), BF16),
            rep_sems,
            own_sems,
            rep_sems,
            own_sems,
            rep_sems,
            rep_sems,
            spread_sems,
            spread_sems,
            pltpu.SemaphoreType.DMA((7,)),
            pltpu.SemaphoreType.DMA((6,)),
        ],
        compiler_params=pltpu.CompilerParams(
            collective_id=0, has_side_effects=True, vmem_limit_bytes=62 * 1024 * 1024
        ),
        name="outer_step",
    )(
        owner_list[None, :],
        jnp.transpose(local_dense[0], (1, 0, 2)).reshape(units * rows, lanes),
        local_embed[0],
        anchor_embed,
        projection.T,
        moment_embed.T,
        turn_slots(anchor_slots),
        turn_slots(moment_slots),
    )

    size = round_up(-(-sent // steps), 64)

    def part_of(shape):
        return pl.BlockSpec((shape[0] // steps,) + shape[1:], lambda step: (step, 0))

    plain = [part_of(one.shape) for one in rest]
    dense, embed_weights, anchor_new, moment_new, anchor_embed_new, moment_embed_new = pl.pallas_call(
        functools.partial(finish_kernel, cols),
        grid=(steps,),
        out_shape=(
            jax.ShapeDtypeStruct((units * rows, lanes), BF16),
            jax.ShapeDtypeStruct((vocab, features), BF16),
        )
        + tuple(jax.ShapeDtypeStruct(one.shape, F32) for one in rest),
        in_specs=[
            pl.BlockSpec((reps, size, lanes), lambda step: (0, step, 0)),
            pl.BlockSpec((reps, vocab // steps, lanes), lambda step: (0, step, 0)),
        ]
        + plain,
        out_specs=[
            pl.BlockSpec((size * reps, lanes), lambda step: (step, 0)),
            pl.BlockSpec((vocab // steps, features), lambda step: (step, 0)),
        ]
        + plain,
        scratch_shapes=[
            pltpu.VMEM((reps * lanes, reps * lanes), BF16),
            pltpu.VMEM((size * reps, lanes), F32),
        ],
        name="outer_step_finish",
    )(column, embed_new, *rest)
    return (
        jnp.transpose(dense.reshape(units, rows, lanes), (1, 0, 2)),
        unturn_slots(anchor_new),
        unturn_slots(moment_new),
        embed_weights,
        anchor_embed_new,
        moment_embed_new.T,
    )


def solution(mesh):
    placed = (
        P("rep", "own", None, None),
        P(),
        P("own", None, None, "rep"),
        P("own", None, None, "rep"),
        P("rep", "own", None),
        P("own", "rep"),
        P("own", None),
        P(),
    )
    return jax.shard_map(
        on_device,
        mesh=mesh,
        in_specs=placed,
        out_specs=(
            P("own", None, None),
            P("own", None, None, "rep"),
            P("own", None, None, "rep"),
            P("own", None),
            P("own", "rep"),
            P("own", None),
        ),
        check_vma=False,
    )
```

```python
import functools

import jax
import jax.numpy as jnp
from jax import lax
from jax.experimental import pallas as pl
from jax.experimental.pallas import tpu as pltpu
from jax.sharding import PartitionSpec as P

OUTER_MOMENTUM = 0.9
OUTER_RATE = 0.7
CLIP_RMS = 2.0
EPSILON = 1e-06
MESH = pl.DeviceIdType.MESH
F32 = jnp.float32
BF16 = jnp.bfloat16
HIGHEST = lax.Precision.HIGHEST


def iota(shape, axis):
    return lax.broadcasted_iota(jnp.int32, shape, axis)


def onehot(condition):
    return jnp.where(condition, 1.0, 0.0).astype(BF16)


def swap_matrix(reps, cols):
    lanes = reps * cols
    at = iota((reps * lanes, 1), 0)
    to = ((at // cols) % reps) * lanes + (at // lanes) * cols + at % cols
    return onehot(iota((reps * lanes, reps * lanes), 1) == to)


def kernel(
    dims,
    owner_ref,
    dense_hbm,
    embed_hbm,
    anchor_embed_hbm,
    projection_hbm,
    moment_embed_hbm,
    anchor_hbm,
    moment_hbm,
    column_out,
    embed_out,
    anchor_out,
    moment_out,
    anchor_embed_out,
    moment_embed_out,
    dense_ref,
    embed_ref,
    anchor_embed_ref,
    projection_ref,
    moment_embed_ref,
    anchor_ref,
    moment_ref,
    anchor_new_ref,
    moment_new_ref,
    anchor_embed_new_ref,
    moment_embed_new_ref,
    swap,
    stored,
    wide,
    share_send,
    far_recv,
    near_recv,
    joined_send,
    joined_recv,
    cross_send,
    cross_recv,
    summed,
    slot_pick,
    unit_pick,
    to_rows,
    from_rows,
    out_send,
    out_recv,
    slots_f32,
    spread,
    change,
    squares_send,
    squares_recv,
    back_send,
    back_recv,
    column_send,
    part_send,
    part_recv,
    part_sum,
    compressed,
    embed_send,
    share_sems,
    out_sems,
    squares_sems,
    back_sems,
    part_sems,
    compressed_sems,
    column_sems,
    embed_sems,
    in_sems,
    local_sems,
):
    reps, owners, units, rows, cap, cols = dims
    lanes = reps * cols
    quads = rows // reps
    real = units * quads
    sent = share_send.shape[2]
    padded = summed.shape[0]
    block = quads * cap
    sources = owners * quads
    ring = reps // 2
    me_rep = lax.axis_index("rep")
    me_own = lax.axis_index("own")
    side = me_rep // ring
    place = lax.rem(me_rep, ring)

    def rep_at(flip, move):
        return lax.rem(side + flip, 2) * ring + lax.rem(place + move, ring)

    def rep_peer(step):
        return rep_at(step // ring, lax.rem(step, ring))

    def rep_source(step):
        return rep_at(step // ring, ring - lax.rem(step, ring))

    def own_peer(step):
        return lax.rem(me_own + step, owners)

    def own_source(step):
        return lax.rem(me_own + owners - step, owners)

    def send(src, dst, sems, index, device):
        return pltpu.make_async_remote_copy(
            src_ref=src,
            dst_ref=dst,
            send_sem=sems.at[0, index],
            recv_sem=sems.at[1, index],
            device_id=device,
            device_id_type=MESH,
        )

    def rep_copy(src, dst, sems, step):
        return send(src, dst, sems, step - 1, (rep_peer(step), me_own))

    def own_copy(src, dst, sems, step):
        return send(src, dst, sems, step - 1, (me_rep, own_peer(step)))

    def loop(count, body):
        def run(step, carry):
            body(step)
            return carry

        lax.fori_loop(0, count, run, 0)

    def rep_loop(body):
        loop(reps - 1, lambda step: body(step + 1))

    def own_loop(body):
        loop(owners - 1, lambda step: body(step + 1))

    def aligned(start, size, by):
        return pl.ds(pl.multiple_of(start, by), size)

    class Spread:
        def __init__(self, own, slots, sems):
            half = slots.shape[1] // 2 // 16 * 16
            first = pl.ds(0, half)
            second = pl.ds(half, slots.shape[1] - half)
            up, down, over = rep_at(0, 1), rep_at(0, ring - 1), rep_at(1, 0)
            over_up, over_down = rep_at(1, 1), rep_at(1, ring - 1)
            far, over_far = rep_at(0, 2), rep_at(1, 2)
            self.own_slot = slots.at[me_rep]
            self.own = own
            self.sems = sems
            self.sends = [
                (own, slots.at[me_rep], over),
                (own, slots.at[me_rep], up),
                (own, slots.at[me_rep], down),
                (slots.at[over], slots.at[over], up),
                (slots.at[over], slots.at[over], down),
                (slots.at[down, first], slots.at[down, first], up),
                (slots.at[up, second], slots.at[up, second], down),
                (slots.at[over_down, first], slots.at[over_down, first], up),
                (slots.at[over_up, second], slots.at[over_up, second], down),
            ]
            self.lands = [
                slots.at[over],
                slots.at[down],
                slots.at[up],
                slots.at[over_down],
                slots.at[over_up],
                slots.at[far, first],
                slots.at[far, second],
                slots.at[over_far, first],
                slots.at[over_far, second],
            ]

        def copy(self, index):
            src, dst, device = self.sends[index]
            return send(src, dst, self.sems, index, (device, me_own))

        def start(self, *indices):
            for index in indices:
                self.copy(index).start()

        def arrived(self, *indices):
            for index in indices:
                land = self.lands[index]
                send(land, land, self.sems, index, (rep_at(1, 0), me_own)).wait_recv()

        def finish(self):
            for index in range(len(self.sends)):
                self.copy(index).wait_send()

    def fetch(index, src, dst):
        return pltpu.make_async_copy(src, dst, in_sems.at[index])

    fetches = [
        fetch(0, dense_hbm, dense_ref),
        fetch(1, embed_hbm, embed_ref),
        fetch(2, anchor_embed_hbm, anchor_embed_ref),
        fetch(3, projection_hbm, projection_ref),
        fetch(4, moment_embed_hbm, moment_embed_ref),
        fetch(5, anchor_hbm, anchor_ref),
        fetch(6, moment_hbm, moment_ref),
    ]
    for one in fetches:
        one.start()

    barrier = pltpu.get_barrier_semaphore()
    rep_loop(
        lambda step: pl.semaphore_signal(
            barrier, inc=1, device_id=(rep_peer(step), me_own), device_id_type=MESH
        )
    )
    own_loop(
        lambda step: pl.semaphore_signal(
            barrier, inc=1, device_id=(me_rep, own_peer(step)), device_id_type=MESH
        )
    )

    swap[...] = swap_matrix(reps, cols)
    row_count = dense_ref.shape[0]
    fetches[0].wait()
    stored[pl.ds(0, row_count), :] = dense_ref[...].astype(F32)
    stored[pl.ds(row_count, padded * reps - row_count), :] = jnp.zeros(
        (padded * reps - row_count, lanes), F32
    )
    for group in range(reps):
        wide[:, group * lanes : (group + 1) * lanes] = stored[
            pl.ds(group, padded, stride=reps), :
        ].astype(BF16)

    def share_of(which):
        return jnp.dot(
            wide[...], swap[:, aligned(which * lanes, lanes, lanes)], preferred_element_type=F32
        )[:sent]

    up, down = 1, ring - 1
    cut = sent // 2 // 16 * 16
    upper, lower = pl.ds(0, cut), pl.ds(cut, sent - cut)
    FAR, UP, DOWN, SELF = range(4)

    def hop(turn, index):
        src, dst, part, move = (
            (share_send.at[turn, FAR], far_recv, upper, up),
            (share_send.at[turn, FAR], far_recv, lower, down),
            (share_send.at[turn, UP], near_recv, lower, up),
            (share_send.at[turn, DOWN], near_recv, upper, down),
            (joined_send.at[turn], joined_recv, upper, up),
            (joined_send.at[turn], joined_recv, lower, down),
        )[index]
        return send(
            src.at[part], dst.at[turn, part], share_sems, turn * 6 + index, (rep_at(0, move), me_own)
        )

    def cross():
        return send(cross_send, cross_recv, share_sems, 12, (rep_at(1, 0), me_own))

    def pack(turn, kind):
        move = (2, up, down, 0)[kind]
        share_send[turn, kind] = share_of(rep_at(1 - turn, move)).astype(BF16)

    def join(turn, index, part, kind):
        hop(turn, index).wait_recv()
        joined_send[turn, part, :] = (
            far_recv[turn, part, :].astype(F32) + share_send[turn, kind, part, :].astype(F32)
        ).astype(BF16)
        hop(turn, index + 4).start()

    def ring_total(turn):
        for index in range(2, 6):
            hop(turn, index).wait_recv()
        return (
            share_send[turn, SELF].astype(F32)
            + near_recv[turn].astype(F32)
            + joined_recv[turn].astype(F32)
        )

    pack(0, FAR)
    pl.semaphore_wait(barrier, reps - 1 + owners - 1)
    hop(0, 0).start()
    hop(0, 1).start()
    pack(0, UP)
    hop(0, 2).start()
    pack(0, DOWN)
    hop(0, 3).start()
    pack(1, FAR)
    hop(1, 0).start()
    hop(1, 1).start()
    pack(0, SELF)
    join(0, 0, upper, UP)
    join(0, 1, lower, DOWN)
    pack(1, UP)
    hop(1, 2).start()
    pack(1, DOWN)
    hop(1, 3).start()
    pack(1, SELF)
    join(1, 0, upper, UP)
    join(1, 1, lower, DOWN)
    cross_send[...] = ring_total(0).astype(BF16)
    cross().start()

    for one in fetches[1:]:
        one.wait()
    my_projection = projection_ref[:, aligned(me_rep * lanes, lanes, lanes)].astype(F32)
    last = (((1,), (1,)), ((), ()))
    part = lax.dot_general(
        my_projection, anchor_embed_ref[...], last, precision=HIGHEST, preferred_element_type=F32
    )
    part_send[...] = part - lax.dot_general(
        projection_ref[...], embed_ref[...], last, preferred_element_type=F32
    ) / reps
    ranks = part_send.shape[0] // reps

    def part_copy(step):
        return rep_copy(
            part_send.at[aligned(rep_peer(step) * ranks, ranks, 8)], part_recv.at[step - 1], part_sems, step
        )

    rep_loop(lambda step: part_copy(step).start())

    owners_of = owner_ref[...].astype(F32)
    expand = onehot(iota((units, padded), 0) == iota((units, padded), 1) // quads)
    owner_row = jnp.dot(
        jnp.broadcast_to(owners_of, (8, units)).astype(BF16), expand, preferred_element_type=F32
    )[0:1].astype(jnp.int32)
    owner_col = jnp.sum(
        jnp.where(iota((padded, units), 1) == iota((padded, units), 0) // quads, owners_of, 0.0),
        axis=1,
        keepdims=True,
    ).astype(jnp.int32)

    def targets(owner_at, owner_over, at_axis):
        shape = (padded, padded)
        at = iota(shape, at_axis)
        over = iota(shape, 1 - at_axis)
        before = (owner_at == owner_over) & (over < at) & (over % quads == at % quads)
        rank = jnp.sum(jnp.where(before, 1.0, 0.0), axis=1 - at_axis, keepdims=True).astype(jnp.int32)
        short = (1, padded) if at_axis == 1 else (padded, 1)
        quad = iota(short, at_axis)
        target = owner_at * block + (quad % quads) * cap + rank
        return jnp.where(quad < real, target, -1)

    row_targets = targets(owner_row, owner_col, 1)
    col_targets = targets(owner_col, owner_row, 0)
    slot_rows = slot_pick.shape[0]
    slot_pick[...] = onehot(iota((slot_rows, padded), 0) == row_targets)
    unit_pick[...] = onehot(iota((padded, slot_rows), 1) == col_targets)
    held = jnp.sum(
        jnp.where((owner_row == me_own) & (iota((1, padded), 1) < real), 1.0, 0.0), axis=1, keepdims=True
    )
    width = sources * reps
    at = iota((width, 1), 0)
    to = iota((width, width), 1)
    to_rows[...] = onehot((at % sources) * reps + at // sources == to)
    from_rows[...] = onehot((at % reps) * sources + at // reps == to)

    share_total = ring_total(1)
    cross().wait_recv()
    share_total = share_total + cross_recv[...].astype(F32)
    summed[pl.ds(0, sent), :] = share_total.astype(BF16)
    summed[pl.ds(sent, padded - sent), :] = jnp.zeros((padded - sent, lanes), BF16)
    out_send[...] = jnp.dot(slot_pick[...], summed[...], preferred_element_type=F32).astype(BF16)

    def own_block(index):
        return aligned(index * block, block, 16)

    def out_copy(step, source):
        return own_copy(
            out_send.at[own_block(own_peer(step))], out_recv.at[own_block(source)], out_sems, step
        )

    own_loop(lambda step: out_copy(step, me_own).start())
    out_recv[own_block(me_own), :] = out_send[own_block(me_own), :]

    my_ranks = aligned(me_rep * ranks, ranks, 8)
    rep_loop(lambda step: part_copy(step).wait_recv())
    total = part_send[my_ranks, :]
    for step in range(1, reps):
        total = total + part_recv[step - 1]
    part_sum[...] = total
    compressed[my_ranks, :] = total

    def compressed_copy(step, source):
        return rep_copy(part_sum, compressed.at[aligned(source * ranks, ranks, 8)], compressed_sems, step)

    rep_loop(lambda step: compressed_copy(step, me_rep).start())
    rep_loop(lambda step: compressed_copy(step, rep_source(step)).wait_recv())
    change_embed = compressed[...]
    moment_embed_new = OUTER_MOMENTUM * moment_embed_ref[...] + change_embed
    moment_embed_new_ref[...] = moment_embed_new
    first = (((0,), (0,)), ((), ()))
    anchor_embed_new = anchor_embed_ref[...] - OUTER_RATE * lax.dot_general(
        change_embed + OUTER_MOMENTUM * moment_embed_new,
        my_projection,
        first,
        precision=HIGHEST,
        preferred_element_type=F32,
    )
    anchor_embed_new_ref[...] = anchor_embed_new
    embed_send[...] = anchor_embed_new.astype(BF16)
    embed_spread = Spread(embed_send, embed_out, embed_sems)
    embed_spread.start(0, 1, 2)

    def store(index, src, dst):
        return pltpu.make_async_copy(src, dst, local_sems.at[index])

    stores = [
        store(0, embed_send, embed_spread.own_slot),
        store(1, anchor_embed_new_ref, anchor_embed_out),
        store(2, moment_embed_new_ref, moment_embed_out),
    ]
    for one in stores:
        one.start()

    own_loop(lambda step: out_copy(step, own_source(step)).wait_recv())
    slots_f32[...] = out_recv[...].astype(F32)
    for slot in range(cap):
        turned = slots_f32[pl.ds(slot, sources, stride=cap), :].T
        for group in range(reps):
            spread[slot * cols : (slot + 1) * cols, group * sources : (group + 1) * sources] = turned[
                group * cols : (group + 1) * cols
            ].astype(BF16)
    owned = jnp.dot(spread[...], to_rows[...], preferred_element_type=F32)
    change[...] = anchor_ref[...] - owned / reps
    squares_send[...] = jnp.zeros_like(squares_send)
    for slot in range(cap):
        one = change[slot * cols : (slot + 1) * cols, :]
        total = jnp.sum(jnp.sum(one * one, axis=0, keepdims=True), axis=1, keepdims=True)
        squares_send[slot : slot + 1, :] = jnp.broadcast_to(total, (1, squares_send.shape[1]))

    def squares_copy(step):
        return rep_copy(squares_send, squares_recv.at[step - 1], squares_sems, step)

    rep_loop(lambda step: squares_copy(step).start())
    embed_spread.arrived(0, 1, 2)
    embed_spread.start(3, 4, 5, 6)
    rep_loop(lambda step: squares_copy(step).wait_recv())
    squares = squares_send[...]
    for step in range(1, reps):
        squares = squares + squares_recv[step - 1]
    root_mean = jnp.sqrt(squares / (owners * rows * lanes) + EPSILON)
    factors = jnp.minimum(1.0, CLIP_RMS / root_mean)
    for slot in range(cap):
        at = pl.ds(slot * cols, cols)
        live = jnp.where(held > slot * quads, 1.0, 0.0)
        clipped = change[at, :] * factors[slot : slot + 1, 0:1]
        moment_new = live * (OUTER_MOMENTUM * moment_ref[at, :] + clipped)
        anchor_new = live * (anchor_ref[at, :] - OUTER_RATE * (clipped + OUTER_MOMENTUM * moment_new))
        moment_new_ref[at, :] = moment_new
        anchor_new_ref[at, :] = anchor_new
        spread[at, :] = anchor_new.astype(BF16)
    regrouped = jnp.dot(spread[...], from_rows[...], preferred_element_type=F32)
    for slot in range(cap):
        turned = jnp.concatenate(
            [
                regrouped[slot * cols : (slot + 1) * cols, group * sources : (group + 1) * sources]
                for group in range(reps)
            ],
            axis=0,
        ).T
        slots_f32[pl.ds(slot, sources, stride=cap), :] = turned
    back_send[...] = slots_f32[...].astype(BF16)

    def back_copy(step, source):
        return own_copy(
            back_send.at[own_block(own_peer(step))], back_recv.at[own_block(source)], back_sems, step
        )

    own_loop(lambda step: back_copy(step, me_own).start())
    back_recv[own_block(me_own), :] = back_send[own_block(me_own), :]
    late = [store(3, anchor_new_ref, anchor_out), store(4, moment_new_ref, moment_out)]
    for one in late:
        one.start()
    embed_spread.arrived(3, 4)
    embed_spread.start(7, 8)
    own_loop(lambda step: back_copy(step, own_source(step)).wait_recv())

    column_send[...] = jnp.dot(unit_pick[...], back_recv[...], preferred_element_type=F32)[:sent].astype(BF16)
    column_spread = Spread(column_send, column_out, column_sems)
    column_spread.start(0, 1, 2)
    late.append(store(5, column_send, column_spread.own_slot))
    late[-1].start()
    column_spread.arrived(0)
    column_spread.start(3, 4)
    column_spread.arrived(1)
    column_spread.start(5)
    column_spread.arrived(2)
    column_spread.start(6)
    column_spread.arrived(3)
    column_spread.start(7)
    column_spread.arrived(4)
    column_spread.start(8)

    for one in stores + late:
        one.wait()
    embed_spread.arrived(5, 6, 7, 8)
    embed_spread.finish()
    rep_loop(lambda step: part_copy(step).wait_send())
    for index in range(6):
        hop(0, index).wait_send()
        hop(1, index).wait_send()
    cross().wait_send()
    rep_loop(lambda step: compressed_copy(step, me_rep).wait_send())
    rep_loop(lambda step: squares_copy(step).wait_send())
    own_loop(lambda step: out_copy(step, me_own).wait_send())
    own_loop(lambda step: back_copy(step, me_own).wait_send())
    column_spread.arrived(5, 6, 7, 8)
    column_spread.finish()


def finish_kernel(
    cols,
    column_ref,
    embed_ref,
    anchor_ref,
    moment_ref,
    anchor_embed_ref,
    moment_embed_ref,
    dense_out,
    embed_out,
    anchor_out,
    moment_out,
    anchor_embed_out,
    moment_embed_out,
    swap,
    stored,
):
    reps, size, lanes = column_ref.shape

    @pl.when(pl.program_id(0) == 0)
    def _():
        swap[...] = swap_matrix(reps, cols)

    gathered = jnp.concatenate([column_ref[group] for group in range(reps)], axis=1)
    ordered = jnp.dot(gathered, swap[...], preferred_element_type=F32)
    for group in range(reps):
        stored[pl.ds(group, size, stride=reps), :] = ordered[:, group * lanes : (group + 1) * lanes]
    dense_out[...] = stored[...].astype(BF16)
    for group in range(reps):
        embed_out[:, group * lanes : (group + 1) * lanes] = embed_ref[group]
    anchor_out[...] = anchor_ref[...]
    moment_out[...] = moment_ref[...]
    anchor_embed_out[...] = anchor_embed_ref[...]
    moment_embed_out[...] = moment_embed_ref[...]


def round_up(value, to):
    return -(-value // to) * to


def on_device(
    local_dense,
    owner_list,
    anchor_slots,
    moment_slots,
    local_embed,
    anchor_embed,
    moment_embed,
    projection,
):
    owners = lax.axis_size("own")
    reps = lax.axis_size("rep")
    _, rows, units, lanes = local_dense.shape
    _, width, cap, cols = anchor_slots.shape
    vocab, rank = moment_embed.shape
    features = projection.shape[0]
    quads = rows // reps
    real = units * quads
    sent = round_up(real, 16)
    padded = round_up(real, 128)
    block = quads * cap
    slot_rows = owners * block
    slot_cols = cap * cols
    steps = 2

    def turn_slots(slots):
        return jnp.transpose(slots[0], (1, 2, 0)).reshape(slot_cols, width)

    def unturn_slots(slots):
        return jnp.transpose(slots.reshape(cap, cols, width), (2, 0, 1))[None]

    vmem = pl.BlockSpec(memory_space=pltpu.VMEM)
    anywhere = pl.BlockSpec(memory_space=pl.ANY)
    rep_sems = pltpu.SemaphoreType.DMA((2, reps - 1))
    own_sems = pltpu.SemaphoreType.DMA((2, owners - 1))
    spread_sems = pltpu.SemaphoreType.DMA((2, 9))
    slot_shape = pltpu.VMEM((slot_cols, width), F32)
    ring_shape = pltpu.VMEM((2, sent, lanes), BF16)
    column, embed_new, *rest = pl.pallas_call(
        functools.partial(kernel, (reps, owners, units, rows, cap, cols)),
        out_shape=(
            jax.ShapeDtypeStruct((reps, sent, lanes), BF16),
            jax.ShapeDtypeStruct((reps, vocab, lanes), BF16),
            jax.ShapeDtypeStruct((slot_cols, width), F32),
            jax.ShapeDtypeStruct((slot_cols, width), F32),
            jax.ShapeDtypeStruct((vocab, lanes), F32),
            jax.ShapeDtypeStruct((rank, vocab), F32),
        ),
        in_specs=[vmem] + [anywhere] * 7,
        out_specs=(anywhere,) * 6,
        scratch_shapes=[
            pltpu.VMEM((units * rows, lanes), BF16),
            pltpu.VMEM((vocab, features), BF16),
            pltpu.VMEM((vocab, lanes), F32),
            pltpu.VMEM((rank, features), BF16),
            pltpu.VMEM((rank, vocab), F32),
            slot_shape,
            slot_shape,
            slot_shape,
            slot_shape,
            pltpu.VMEM((vocab, lanes), F32),
            pltpu.VMEM((rank, vocab), F32),
            pltpu.VMEM((reps * lanes, reps * lanes), BF16),
            pltpu.VMEM((padded * reps, lanes), F32),
            pltpu.VMEM((padded, reps * lanes), BF16),
            pltpu.VMEM((2, 4, sent, lanes), BF16),
            ring_shape,
            ring_shape,
            ring_shape,
            ring_shape,
            pltpu.VMEM((sent, lanes), BF16),
            pltpu.VMEM((sent, lanes), BF16),
            pltpu.VMEM((padded, lanes), BF16),
            pltpu.VMEM((slot_rows, padded), BF16),
            pltpu.VMEM((padded, slot_rows), BF16),
            pltpu.VMEM((width, width), BF16),
            pltpu.VMEM((width, width), BF16),
            pltpu.VMEM((slot_rows, lanes), BF16),
            pltpu.VMEM((slot_rows, lanes), BF16),
            pltpu.VMEM((slot_rows, lanes), F32),
            pltpu.VMEM((slot_cols, width), BF16),
            slot_shape,
            pltpu.VMEM((round_up(cap, 8), lanes), F32),
            pltpu.VMEM((reps - 1, round_up(cap, 8), lanes), F32),
            pltpu.VMEM((slot_rows, lanes), BF16),
            pltpu.VMEM((slot_rows, lanes), BF16),
            pltpu.VMEM((sent, lanes), BF16),
            pltpu.VMEM((rank, vocab), F32),
            pltpu.VMEM((reps - 1, rank // reps, vocab), F32),
            pltpu.VMEM((rank // reps, vocab), F32),
            pltpu.VMEM((rank, vocab), F32),
            pltpu.VMEM((vocab, lanes), BF16),
            pltpu.SemaphoreType.DMA((2, 13)),
            own_sems,
            rep_sems,
            own_sems,
            rep_sems,
            rep_sems,
            spread_sems,
            spread_sems,
            pltpu.SemaphoreType.DMA((7,)),
            pltpu.SemaphoreType.DMA((6,)),
        ],
        compiler_params=pltpu.CompilerParams(
            collective_id=0, has_side_effects=True, vmem_limit_bytes=62 * 1024 * 1024
        ),
        name="outer_step",
    )(
        owner_list[None, :],
        jnp.transpose(local_dense[0], (1, 0, 2)).reshape(units * rows, lanes),
        local_embed[0],
        anchor_embed,
        projection.T,
        moment_embed.T,
        turn_slots(anchor_slots),
        turn_slots(moment_slots),
    )

    size = round_up(-(-sent // steps), 64)

    def part_of(shape):
        return pl.BlockSpec((shape[0] // steps,) + shape[1:], lambda step: (step, 0))

    plain = [part_of(one.shape) for one in rest]
    dense, embed_weights, anchor_new, moment_new, anchor_embed_new, moment_embed_new = pl.pallas_call(
        functools.partial(finish_kernel, cols),
        grid=(steps,),
        out_shape=(
            jax.ShapeDtypeStruct((units * rows, lanes), BF16),
            jax.ShapeDtypeStruct((vocab, features), BF16),
        )
        + tuple(jax.ShapeDtypeStruct(one.shape, F32) for one in rest),
        in_specs=[
            pl.BlockSpec((reps, size, lanes), lambda step: (0, step, 0)),
            pl.BlockSpec((reps, vocab // steps, lanes), lambda step: (0, step, 0)),
        ]
        + plain,
        out_specs=[
            pl.BlockSpec((size * reps, lanes), lambda step: (step, 0)),
            pl.BlockSpec((vocab // steps, features), lambda step: (step, 0)),
        ]
        + plain,
        scratch_shapes=[
            pltpu.VMEM((reps * lanes, reps * lanes), BF16),
            pltpu.VMEM((size * reps, lanes), F32),
        ],
        name="outer_step_finish",
    )(column, embed_new, *rest)
    return (
        jnp.transpose(dense.reshape(units, rows, lanes), (1, 0, 2)),
        unturn_slots(anchor_new),
        unturn_slots(moment_new),
        embed_weights,
        anchor_embed_new,
        moment_embed_new.T,
    )


def solution(mesh):
    placed = (
        P("rep", "own", None, None),
        P(),
        P("own", None, None, "rep"),
        P("own", None, None, "rep"),
        P("rep", "own", None),
        P("own", "rep"),
        P("own", None),
        P(),
    )
    return jax.shard_map(
        on_device,
        mesh=mesh,
        in_specs=placed,
        out_specs=(
            P("own", None, None),
            P("own", None, None, "rep"),
            P("own", None, None, "rep"),
            P("own", None),
            P("own", "rep"),
            P("own", None),
        ),
        check_vma=False,
    )
```

```python
import functools

import jax
import jax.numpy as jnp
from jax import lax
from jax.experimental import pallas as pl
from jax.experimental.pallas import tpu as pltpu
from jax.sharding import PartitionSpec as P

OUTER_MOMENTUM = 0.9
OUTER_RATE = 0.7
CLIP_RMS = 2.0
EPSILON = 1e-06
MESH = pl.DeviceIdType.MESH
F32 = jnp.float32
BF16 = jnp.bfloat16
HIGHEST = lax.Precision.HIGHEST


def iota(shape, axis):
    return lax.broadcasted_iota(jnp.int32, shape, axis)


def onehot(condition):
    return jnp.where(condition, 1.0, 0.0).astype(BF16)


def swap_matrix(reps, cols):
    lanes = reps * cols
    at = iota((reps * lanes, 1), 0)
    to = ((at // cols) % reps) * lanes + (at // lanes) * cols + at % cols
    return onehot(iota((reps * lanes, reps * lanes), 1) == to)


def kernel(
    dims,
    owner_ref,
    dense_hbm,
    embed_hbm,
    anchor_embed_hbm,
    projection_hbm,
    moment_embed_hbm,
    anchor_hbm,
    moment_hbm,
    column_out,
    embed_out,
    anchor_out,
    moment_out,
    anchor_embed_out,
    moment_embed_out,
    dense_ref,
    embed_ref,
    anchor_embed_ref,
    projection_ref,
    moment_embed_ref,
    anchor_ref,
    moment_ref,
    anchor_new_ref,
    moment_new_ref,
    anchor_embed_new_ref,
    moment_embed_new_ref,
    swap,
    stored,
    wide,
    share_send,
    far_recv,
    near_recv,
    joined_send,
    joined_recv,
    cross_send,
    cross_recv,
    summed,
    slot_pick,
    unit_pick,
    to_rows,
    from_rows,
    out_send,
    out_recv,
    slots_f32,
    spread,
    change,
    squares_send,
    squares_recv,
    back_send,
    back_recv,
    column_send,
    part_send,
    part_recv,
    part_sum,
    compressed,
    embed_send,
    share_sems,
    out_sems,
    squares_sems,
    back_sems,
    part_sems,
    compressed_sems,
    column_sems,
    embed_sems,
    in_sems,
    local_sems,
):
    reps, owners, units, rows, cap, cols = dims
    lanes = reps * cols
    quads = rows // reps
    real = units * quads
    sent = share_send.shape[2]
    padded = summed.shape[0]
    block = quads * cap
    sources = owners * quads
    ring = reps // 2
    me_rep = lax.axis_index("rep")
    me_own = lax.axis_index("own")
    side = me_rep // ring
    place = lax.rem(me_rep, ring)

    def rep_at(flip, move):
        return lax.rem(side + flip, 2) * ring + lax.rem(place + move, ring)

    def rep_peer(step):
        return rep_at(step // ring, lax.rem(step, ring))

    def rep_source(step):
        return rep_at(step // ring, ring - lax.rem(step, ring))

    def own_peer(step):
        return lax.rem(me_own + step, owners)

    def own_source(step):
        return lax.rem(me_own + owners - step, owners)

    def send(src, dst, sems, index, device):
        return pltpu.make_async_remote_copy(
            src_ref=src,
            dst_ref=dst,
            send_sem=sems.at[0, index],
            recv_sem=sems.at[1, index],
            device_id=device,
            device_id_type=MESH,
        )

    def rep_copy(src, dst, sems, step):
        return send(src, dst, sems, step - 1, (rep_peer(step), me_own))

    def own_copy(src, dst, sems, step):
        return send(src, dst, sems, step - 1, (me_rep, own_peer(step)))

    def loop(count, body):
        def run(step, carry):
            body(step)
            return carry

        lax.fori_loop(0, count, run, 0)

    def rep_loop(body):
        loop(reps - 1, lambda step: body(step + 1))

    def own_loop(body):
        loop(owners - 1, lambda step: body(step + 1))

    def aligned(start, size, by):
        return pl.ds(pl.multiple_of(start, by), size)

    class Spread:
        def __init__(self, own, slots, sems):
            half = slots.shape[1] // 2 // 16 * 16
            first = pl.ds(0, half)
            second = pl.ds(half, slots.shape[1] - half)
            up, down, over = rep_at(0, 1), rep_at(0, ring - 1), rep_at(1, 0)
            over_up, over_down = rep_at(1, 1), rep_at(1, ring - 1)
            far, over_far = rep_at(0, 2), rep_at(1, 2)
            self.own_slot = slots.at[me_rep]
            self.own = own
            self.sems = sems
            self.sends = [
                (own, slots.at[me_rep], over),
                (own.at[first], slots.at[me_rep, first], up),
                (own.at[second], slots.at[me_rep, second], down),
                (slots.at[over, first], slots.at[over, first], up),
                (slots.at[over, second], slots.at[over, second], down),
                (slots.at[down, first], slots.at[down, first], up),
                (slots.at[up, second], slots.at[up, second], down),
                (slots.at[over_down, first], slots.at[over_down, first], up),
                (slots.at[over_up, second], slots.at[over_up, second], down),
                (own.at[second], slots.at[me_rep, second], up),
                (own.at[first], slots.at[me_rep, first], down),
                (slots.at[over, second], slots.at[over, second], up),
                (slots.at[over, first], slots.at[over, first], down),
            ]
            self.lands = [
                slots.at[over],
                slots.at[down, first],
                slots.at[up, second],
                slots.at[over_down, first],
                slots.at[over_up, second],
                slots.at[far, first],
                slots.at[far, second],
                slots.at[over_far, first],
                slots.at[over_far, second],
                slots.at[down, second],
                slots.at[up, first],
                slots.at[over_down, second],
                slots.at[over_up, first],
            ]

        def copy(self, index):
            src, dst, device = self.sends[index]
            return send(src, dst, self.sems, index, (device, me_own))

        def start(self, *indices):
            for index in indices:
                self.copy(index).start()

        def arrived(self, *indices):
            for index in indices:
                land = self.lands[index]
                send(land, land, self.sems, index, (rep_at(1, 0), me_own)).wait_recv()

        def finish(self):
            for index in range(len(self.sends)):
                self.copy(index).wait_send()

    def fetch(index, src, dst):
        return pltpu.make_async_copy(src, dst, in_sems.at[index])

    fetches = [
        fetch(0, dense_hbm, dense_ref),
        fetch(1, embed_hbm, embed_ref),
        fetch(2, anchor_embed_hbm, anchor_embed_ref),
        fetch(3, projection_hbm, projection_ref),
        fetch(4, moment_embed_hbm, moment_embed_ref),
        fetch(5, anchor_hbm, anchor_ref),
        fetch(6, moment_hbm, moment_ref),
    ]
    for one in fetches:
        one.start()

    barrier = pltpu.get_barrier_semaphore()
    rep_loop(
        lambda step: pl.semaphore_signal(
            barrier, inc=1, device_id=(rep_peer(step), me_own), device_id_type=MESH
        )
    )
    own_loop(
        lambda step: pl.semaphore_signal(
            barrier, inc=1, device_id=(me_rep, own_peer(step)), device_id_type=MESH
        )
    )

    swap[...] = swap_matrix(reps, cols)
    row_count = dense_ref.shape[0]
    fetches[0].wait()
    stored[pl.ds(0, row_count), :] = dense_ref[...].astype(F32)
    stored[pl.ds(row_count, padded * reps - row_count), :] = jnp.zeros(
        (padded * reps - row_count, lanes), F32
    )
    for group in range(reps):
        wide[:, group * lanes : (group + 1) * lanes] = stored[
            pl.ds(group, padded, stride=reps), :
        ].astype(BF16)

    def share_of(which):
        return jnp.dot(
            wide[...], swap[:, aligned(which * lanes, lanes, lanes)], preferred_element_type=F32
        )[:sent]

    up, down = 1, ring - 1
    cut = sent // 2 // 16 * 16
    upper, lower = pl.ds(0, cut), pl.ds(cut, sent - cut)
    FAR, UP, DOWN, SELF = range(4)

    def hop(turn, index):
        src, dst, part, move = (
            (share_send.at[turn, FAR], far_recv, upper, up),
            (share_send.at[turn, FAR], far_recv, lower, down),
            (share_send.at[turn, UP], near_recv, lower, up),
            (share_send.at[turn, DOWN], near_recv, upper, down),
            (joined_send.at[turn], joined_recv, upper, up),
            (joined_send.at[turn], joined_recv, lower, down),
        )[index]
        return send(
            src.at[part], dst.at[turn, part], share_sems, turn * 6 + index, (rep_at(0, move), me_own)
        )

    def cross():
        return send(cross_send, cross_recv, share_sems, 12, (rep_at(1, 0), me_own))

    def pack(turn, kind):
        move = (2, up, down, 0)[kind]
        share_send[turn, kind] = share_of(rep_at(1 - turn, move)).astype(BF16)

    def join(turn, index, part, kind):
        hop(turn, index).wait_recv()
        joined_send[turn, part, :] = (
            far_recv[turn, part, :].astype(F32) + share_send[turn, kind, part, :].astype(F32)
        ).astype(BF16)
        hop(turn, index + 4).start()

    def ring_total(turn):
        for index in range(2, 6):
            hop(turn, index).wait_recv()
        return (
            share_send[turn, SELF].astype(F32)
            + near_recv[turn].astype(F32)
            + joined_recv[turn].astype(F32)
        )

    pack(0, FAR)
    pl.semaphore_wait(barrier, reps - 1 + owners - 1)
    hop(0, 0).start()
    hop(0, 1).start()
    pack(0, UP)
    hop(0, 2).start()
    pack(0, DOWN)
    hop(0, 3).start()
    pack(1, FAR)
    hop(1, 0).start()
    hop(1, 1).start()
    pack(0, SELF)
    join(0, 0, upper, UP)
    join(0, 1, lower, DOWN)
    pack(1, UP)
    hop(1, 2).start()
    pack(1, DOWN)
    hop(1, 3).start()
    pack(1, SELF)
    join(1, 0, upper, UP)
    join(1, 1, lower, DOWN)
    cross_send[...] = ring_total(0).astype(BF16)
    cross().start()

    for one in fetches[1:]:
        one.wait()
    my_projection = projection_ref[:, aligned(me_rep * lanes, lanes, lanes)].astype(F32)
    last = (((1,), (1,)), ((), ()))
    part = lax.dot_general(
        my_projection, anchor_embed_ref[...], last, precision=HIGHEST, preferred_element_type=F32
    )
    part_send[...] = part - lax.dot_general(
        projection_ref[...], embed_ref[...], last, preferred_element_type=F32
    ) / reps
    ranks = part_send.shape[0] // reps

    def part_copy(step):
        return rep_copy(
            part_send.at[aligned(rep_peer(step) * ranks, ranks, 8)], part_recv.at[step - 1], part_sems, step
        )

    rep_loop(lambda step: part_copy(step).start())

    owners_of = owner_ref[...].astype(F32)
    expand = onehot(iota((units, padded), 0) == iota((units, padded), 1) // quads)
    owner_row = jnp.dot(
        jnp.broadcast_to(owners_of, (8, units)).astype(BF16), expand, preferred_element_type=F32
    )[0:1].astype(jnp.int32)
    owner_col = jnp.sum(
        jnp.where(iota((padded, units), 1) == iota((padded, units), 0) // quads, owners_of, 0.0),
        axis=1,
        keepdims=True,
    ).astype(jnp.int32)

    def targets(owner_at, owner_over, at_axis):
        shape = (padded, padded)
        at = iota(shape, at_axis)
        over = iota(shape, 1 - at_axis)
        before = (owner_at == owner_over) & (over < at) & (over % quads == at % quads)
        rank = jnp.sum(jnp.where(before, 1.0, 0.0), axis=1 - at_axis, keepdims=True).astype(jnp.int32)
        short = (1, padded) if at_axis == 1 else (padded, 1)
        quad = iota(short, at_axis)
        target = owner_at * block + (quad % quads) * cap + rank
        return jnp.where(quad < real, target, -1)

    row_targets = targets(owner_row, owner_col, 1)
    col_targets = targets(owner_col, owner_row, 0)
    slot_rows = slot_pick.shape[0]
    slot_pick[...] = onehot(iota((slot_rows, padded), 0) == row_targets)
    unit_pick[...] = onehot(iota((padded, slot_rows), 1) == col_targets)
    held = jnp.sum(
        jnp.where((owner_row == me_own) & (iota((1, padded), 1) < real), 1.0, 0.0), axis=1, keepdims=True
    )
    width = sources * reps
    at = iota((width, 1), 0)
    to = iota((width, width), 1)
    to_rows[...] = onehot((at % sources) * reps + at // sources == to)
    from_rows[...] = onehot((at % reps) * sources + at // reps == to)

    share_total = ring_total(1)
    cross().wait_recv()
    share_total = share_total + cross_recv[...].astype(F32)
    summed[pl.ds(0, sent), :] = share_total.astype(BF16)
    summed[pl.ds(sent, padded - sent), :] = jnp.zeros((padded - sent, lanes), BF16)
    out_send[...] = jnp.dot(slot_pick[...], summed[...], preferred_element_type=F32).astype(BF16)

    def own_block(index):
        return aligned(index * block, block, 16)

    def out_copy(step, source):
        return own_copy(
            out_send.at[own_block(own_peer(step))], out_recv.at[own_block(source)], out_sems, step
        )

    own_loop(lambda step: out_copy(step, me_own).start())
    out_recv[own_block(me_own), :] = out_send[own_block(me_own), :]

    my_ranks = aligned(me_rep * ranks, ranks, 8)
    rep_loop(lambda step: part_copy(step).wait_recv())
    total = part_send[my_ranks, :]
    for step in range(1, reps):
        total = total + part_recv[step - 1]
    part_sum[...] = total
    compressed[my_ranks, :] = total

    def compressed_copy(step, source):
        return rep_copy(part_sum, compressed.at[aligned(source * ranks, ranks, 8)], compressed_sems, step)

    rep_loop(lambda step: compressed_copy(step, me_rep).start())
    rep_loop(lambda step: compressed_copy(step, rep_source(step)).wait_recv())
    change_embed = compressed[...]
    moment_embed_new = OUTER_MOMENTUM * moment_embed_ref[...] + change_embed
    moment_embed_new_ref[...] = moment_embed_new
    first = (((0,), (0,)), ((), ()))
    anchor_embed_new = anchor_embed_ref[...] - OUTER_RATE * lax.dot_general(
        change_embed + OUTER_MOMENTUM * moment_embed_new,
        my_projection,
        first,
        precision=HIGHEST,
        preferred_element_type=F32,
    )
    anchor_embed_new_ref[...] = anchor_embed_new
    embed_send[...] = anchor_embed_new.astype(BF16)
    embed_spread = Spread(embed_send, embed_out, embed_sems)
    embed_spread.start(0, 1, 2, 9, 10)

    def store(index, src, dst):
        return pltpu.make_async_copy(src, dst, local_sems.at[index])

    stores = [
        store(0, embed_send, embed_spread.own_slot),
        store(1, anchor_embed_new_ref, anchor_embed_out),
        store(2, moment_embed_new_ref, moment_embed_out),
    ]
    for one in stores:
        one.start()

    own_loop(lambda step: out_copy(step, own_source(step)).wait_recv())
    slots_f32[...] = out_recv[...].astype(F32)
    for slot in range(cap):
        turned = slots_f32[pl.ds(slot, sources, stride=cap), :].T
        for group in range(reps):
            spread[slot * cols : (slot + 1) * cols, group * sources : (group + 1) * sources] = turned[
                group * cols : (group + 1) * cols
            ].astype(BF16)
    owned = jnp.dot(spread[...], to_rows[...], preferred_element_type=F32)
    change[...] = anchor_ref[...] - owned / reps
    squares_send[...] = jnp.zeros_like(squares_send)
    for slot in range(cap):
        one = change[slot * cols : (slot + 1) * cols, :]
        total = jnp.sum(jnp.sum(one * one, axis=0, keepdims=True), axis=1, keepdims=True)
        squares_send[slot : slot + 1, :] = jnp.broadcast_to(total, (1, squares_send.shape[1]))

    def squares_copy(step):
        return rep_copy(squares_send, squares_recv.at[step - 1], squares_sems, step)

    rep_loop(lambda step: squares_copy(step).start())
    embed_spread.arrived(0, 1, 2)
    embed_spread.start(3, 4, 11, 12, 5, 6)
    rep_loop(lambda step: squares_copy(step).wait_recv())
    squares = squares_send[...]
    for step in range(1, reps):
        squares = squares + squares_recv[step - 1]
    root_mean = jnp.sqrt(squares / (owners * rows * lanes) + EPSILON)
    factors = jnp.minimum(1.0, CLIP_RMS / root_mean)
    for slot in range(cap):
        at = pl.ds(slot * cols, cols)
        live = jnp.where(held > slot * quads, 1.0, 0.0)
        clipped = change[at, :] * factors[slot : slot + 1, 0:1]
        moment_new = live * (OUTER_MOMENTUM * moment_ref[at, :] + clipped)
        anchor_new = live * (anchor_ref[at, :] - OUTER_RATE * (clipped + OUTER_MOMENTUM * moment_new))
        moment_new_ref[at, :] = moment_new
        anchor_new_ref[at, :] = anchor_new
        spread[at, :] = anchor_new.astype(BF16)
    regrouped = jnp.dot(spread[...], from_rows[...], preferred_element_type=F32)
    for slot in range(cap):
        turned = jnp.concatenate(
            [
                regrouped[slot * cols : (slot + 1) * cols, group * sources : (group + 1) * sources]
                for group in range(reps)
            ],
            axis=0,
        ).T
        slots_f32[pl.ds(slot, sources, stride=cap), :] = turned
    back_send[...] = slots_f32[...].astype(BF16)

    def back_copy(step, source):
        return own_copy(
            back_send.at[own_block(own_peer(step))], back_recv.at[own_block(source)], back_sems, step
        )

    own_loop(lambda step: back_copy(step, me_own).start())
    back_recv[own_block(me_own), :] = back_send[own_block(me_own), :]
    late = [store(3, anchor_new_ref, anchor_out), store(4, moment_new_ref, moment_out)]
    for one in late:
        one.start()
    embed_spread.arrived(3, 4)
    embed_spread.start(7, 8)
    own_loop(lambda step: back_copy(step, own_source(step)).wait_recv())

    column_send[...] = jnp.dot(unit_pick[...], back_recv[...], preferred_element_type=F32)[:sent].astype(BF16)
    column_spread = Spread(column_send, column_out, column_sems)
    column_spread.start(0, 1, 2, 9, 10)
    late.append(store(5, column_send, column_spread.own_slot))
    late[-1].start()
    column_spread.arrived(1)
    column_spread.start(5)
    column_spread.arrived(2)
    column_spread.start(6)
    column_spread.arrived(0)
    column_spread.start(3, 4, 11, 12)
    column_spread.arrived(3)
    column_spread.start(7)
    column_spread.arrived(4)
    column_spread.start(8)

    for one in stores + late:
        one.wait()
    embed_spread.arrived(*range(5, 13))
    embed_spread.finish()
    rep_loop(lambda step: part_copy(step).wait_send())
    for index in range(6):
        hop(0, index).wait_send()
        hop(1, index).wait_send()
    cross().wait_send()
    rep_loop(lambda step: compressed_copy(step, me_rep).wait_send())
    rep_loop(lambda step: squares_copy(step).wait_send())
    own_loop(lambda step: out_copy(step, me_own).wait_send())
    own_loop(lambda step: back_copy(step, me_own).wait_send())
    column_spread.arrived(*range(5, 13))
    column_spread.finish()


def finish_kernel(
    cols,
    column_ref,
    embed_ref,
    anchor_ref,
    moment_ref,
    anchor_embed_ref,
    moment_embed_ref,
    dense_out,
    embed_out,
    anchor_out,
    moment_out,
    anchor_embed_out,
    moment_embed_out,
    swap,
    stored,
):
    reps, size, lanes = column_ref.shape

    @pl.when(pl.program_id(0) == 0)
    def _():
        swap[...] = swap_matrix(reps, cols)

    gathered = jnp.concatenate([column_ref[group] for group in range(reps)], axis=1)
    ordered = jnp.dot(gathered, swap[...], preferred_element_type=F32)
    for group in range(reps):
        stored[pl.ds(group, size, stride=reps), :] = ordered[:, group * lanes : (group + 1) * lanes]
    dense_out[...] = stored[...].astype(BF16)
    for group in range(reps):
        embed_out[:, group * lanes : (group + 1) * lanes] = embed_ref[group]
    anchor_out[...] = anchor_ref[...]
    moment_out[...] = moment_ref[...]
    anchor_embed_out[...] = anchor_embed_ref[...]
    moment_embed_out[...] = moment_embed_ref[...]


def round_up(value, to):
    return -(-value // to) * to


def on_device(
    local_dense,
    owner_list,
    anchor_slots,
    moment_slots,
    local_embed,
    anchor_embed,
    moment_embed,
    projection,
):
    owners = lax.axis_size("own")
    reps = lax.axis_size("rep")
    _, rows, units, lanes = local_dense.shape
    _, width, cap, cols = anchor_slots.shape
    vocab, rank = moment_embed.shape
    features = projection.shape[0]
    quads = rows // reps
    real = units * quads
    sent = round_up(real, 16)
    padded = round_up(real, 128)
    block = quads * cap
    slot_rows = owners * block
    slot_cols = cap * cols
    steps = 2

    def turn_slots(slots):
        return jnp.transpose(slots[0], (1, 2, 0)).reshape(slot_cols, width)

    def unturn_slots(slots):
        return jnp.transpose(slots.reshape(cap, cols, width), (2, 0, 1))[None]

    vmem = pl.BlockSpec(memory_space=pltpu.VMEM)
    anywhere = pl.BlockSpec(memory_space=pl.ANY)
    rep_sems = pltpu.SemaphoreType.DMA((2, reps - 1))
    own_sems = pltpu.SemaphoreType.DMA((2, owners - 1))
    spread_sems = pltpu.SemaphoreType.DMA((2, 13))
    slot_shape = pltpu.VMEM((slot_cols, width), F32)
    ring_shape = pltpu.VMEM((2, sent, lanes), BF16)
    column, embed_new, *rest = pl.pallas_call(
        functools.partial(kernel, (reps, owners, units, rows, cap, cols)),
        out_shape=(
            jax.ShapeDtypeStruct((reps, sent, lanes), BF16),
            jax.ShapeDtypeStruct((reps, vocab, lanes), BF16),
            jax.ShapeDtypeStruct((slot_cols, width), F32),
            jax.ShapeDtypeStruct((slot_cols, width), F32),
            jax.ShapeDtypeStruct((vocab, lanes), F32),
            jax.ShapeDtypeStruct((rank, vocab), F32),
        ),
        in_specs=[vmem] + [anywhere] * 7,
        out_specs=(anywhere,) * 6,
        scratch_shapes=[
            pltpu.VMEM((units * rows, lanes), BF16),
            pltpu.VMEM((vocab, features), BF16),
            pltpu.VMEM((vocab, lanes), F32),
            pltpu.VMEM((rank, features), BF16),
            pltpu.VMEM((rank, vocab), F32),
            slot_shape,
            slot_shape,
            slot_shape,
            slot_shape,
            pltpu.VMEM((vocab, lanes), F32),
            pltpu.VMEM((rank, vocab), F32),
            pltpu.VMEM((reps * lanes, reps * lanes), BF16),
            pltpu.VMEM((padded * reps, lanes), F32),
            pltpu.VMEM((padded, reps * lanes), BF16),
            pltpu.VMEM((2, 4, sent, lanes), BF16),
            ring_shape,
            ring_shape,
            ring_shape,
            ring_shape,
            pltpu.VMEM((sent, lanes), BF16),
            pltpu.VMEM((sent, lanes), BF16),
            pltpu.VMEM((padded, lanes), BF16),
            pltpu.VMEM((slot_rows, padded), BF16),
            pltpu.VMEM((padded, slot_rows), BF16),
            pltpu.VMEM((width, width), BF16),
            pltpu.VMEM((width, width), BF16),
            pltpu.VMEM((slot_rows, lanes), BF16),
            pltpu.VMEM((slot_rows, lanes), BF16),
            pltpu.VMEM((slot_rows, lanes), F32),
            pltpu.VMEM((slot_cols, width), BF16),
            slot_shape,
            pltpu.VMEM((round_up(cap, 8), lanes), F32),
            pltpu.VMEM((reps - 1, round_up(cap, 8), lanes), F32),
            pltpu.VMEM((slot_rows, lanes), BF16),
            pltpu.VMEM((slot_rows, lanes), BF16),
            pltpu.VMEM((sent, lanes), BF16),
            pltpu.VMEM((rank, vocab), F32),
            pltpu.VMEM((reps - 1, rank // reps, vocab), F32),
            pltpu.VMEM((rank // reps, vocab), F32),
            pltpu.VMEM((rank, vocab), F32),
            pltpu.VMEM((vocab, lanes), BF16),
            pltpu.SemaphoreType.DMA((2, 13)),
            own_sems,
            rep_sems,
            own_sems,
            rep_sems,
            rep_sems,
            spread_sems,
            spread_sems,
            pltpu.SemaphoreType.DMA((7,)),
            pltpu.SemaphoreType.DMA((6,)),
        ],
        compiler_params=pltpu.CompilerParams(
            collective_id=0, has_side_effects=True, vmem_limit_bytes=62 * 1024 * 1024
        ),
        name="outer_step",
    )(
        owner_list[None, :],
        jnp.transpose(local_dense[0], (1, 0, 2)).reshape(units * rows, lanes),
        local_embed[0],
        anchor_embed,
        projection.T,
        moment_embed.T,
        turn_slots(anchor_slots),
        turn_slots(moment_slots),
    )

    size = round_up(-(-sent // steps), 64)

    def part_of(shape):
        return pl.BlockSpec((shape[0] // steps,) + shape[1:], lambda step: (step, 0))

    plain = [part_of(one.shape) for one in rest]
    dense, embed_weights, anchor_new, moment_new, anchor_embed_new, moment_embed_new = pl.pallas_call(
        functools.partial(finish_kernel, cols),
        grid=(steps,),
        out_shape=(
            jax.ShapeDtypeStruct((units * rows, lanes), BF16),
            jax.ShapeDtypeStruct((vocab, features), BF16),
        )
        + tuple(jax.ShapeDtypeStruct(one.shape, F32) for one in rest),
        in_specs=[
            pl.BlockSpec((reps, size, lanes), lambda step: (0, step, 0)),
            pl.BlockSpec((reps, vocab // steps, lanes), lambda step: (0, step, 0)),
        ]
        + plain,
        out_specs=[
            pl.BlockSpec((size * reps, lanes), lambda step: (step, 0)),
            pl.BlockSpec((vocab // steps, features), lambda step: (step, 0)),
        ]
        + plain,
        scratch_shapes=[
            pltpu.VMEM((reps * lanes, reps * lanes), BF16),
            pltpu.VMEM((size * reps, lanes), F32),
        ],
        name="outer_step_finish",
    )(column, embed_new, *rest)
    return (
        jnp.transpose(dense.reshape(units, rows, lanes), (1, 0, 2)),
        unturn_slots(anchor_new),
        unturn_slots(moment_new),
        embed_weights,
        anchor_embed_new,
        moment_embed_new.T,
    )


def solution(mesh):
    placed = (
        P("rep", "own", None, None),
        P(),
        P("own", None, None, "rep"),
        P("own", None, None, "rep"),
        P("rep", "own", None),
        P("own", "rep"),
        P("own", None),
        P(),
    )
    return jax.shard_map(
        on_device,
        mesh=mesh,
        in_specs=placed,
        out_specs=(
            P("own", None, None),
            P("own", None, None, "rep"),
            P("own", None, None, "rep"),
            P("own", None),
            P("own", "rep"),
            P("own", None),
        ),
        check_vma=False,
    )
```
